128 devices in a mesh: cells: 128 (over z, y, x, core).
Axes of the slice: x: 4, y: 4, z: 4, core: 2. Of those that a mesh axis runs over, the one named last changes fastest.
Arguments:
- ll_fields: bfloat16 [8, 2097152], P(None, 'cells'), may hold values from -6 to 6
- target: bfloat16 [8, 2097152], P(None, 'cells'), may hold values from -6 to 6
- in_rows: int32 [128, 128, 512], P('cells'), may hold values from 0 to 16383, as said below
- in_slot: int32 [4, 524288], P(None, 'cells'), may hold values from 0 to 65535, as said below
- in_weight: float32 [4, 524288], P(None, 'cells'), may hold values from 0.1 to 0.6
- neighbours: int32 [9, 524288], P(None, 'cells'), may hold values from 0 to 4643, as said below
- conv_weight: bfloat16 [64, 72], replicated, may hold values from -0.75 to 0.75
- up_weight: bfloat16 [256, 64], replicated, may hold values from -0.75 to 0.75
- down_weight: bfloat16 [64, 256], replicated, may hold values from -0.375 to 0.375
- head_weight: bfloat16 [8, 64], replicated, may hold values from -0.75 to 0.75
- out_rows: int32 [128, 128, 512], P('cells'), may hold values from 0 to 4095, as said below
- out_slot: int32 [4, 2097152], P(None, 'cells'), may hold values from 0 to 65535, as said below
- out_weight: float32 [4, 2097152], P(None, 'cells'), may hold values from 0.1 to 0.6
Outputs:
- predicted: bfloat16 [8, 2097152], P(None, 'cells')
- grad_conv: float32 [64, 72], replicated
- grad_up: float32 [256, 64], replicated
- grad_down: float32 [64, 256], replicated
- grad_head: float32 [8, 64], replicated
The draws below stay inside these ranges and needn't reach their ends.
Inputs may be any that keep to these rules, and one draw needn't show every extreme that they name: `in_rows`: local point indices of the sending band. `in_slot`: entry (t, c) is b * 512 + s, a slot received from band b; for each band and tile only the first slots up to a count of 1 to 512 are read, and some slots are read by no cell. `out_rows`: local cell indices of the sending tile. `out_slot`: entry (t, p) is d * 512 + s, a slot received from tile d; for each tile and band only the first slots up to a count of 1 to 512 are read. `neighbours`: positions in the cell's tile bordered by one cell on every side, 18 rows of 258, row major. Entry k names the cell at row offset k // 3 - 1 and column offset k % 3 - 1 from the cell, except at the four corner cells of a tile, where the outward diagonal entry may name the edge neighbour one row away in the same column.
All inputs are finite; a program needn't handle non-finite values.
Results may differ from the reference program's by a relative error of at most 0.0048.
The reference program's roundings to bfloat16 on the way count: a program that leaves them out, or rounds other values in their place, can miss the bound.
Values may be sent and summed in bfloat16 or wider, within the bound.
No kernel may reach another device: no remote copies, remote signals or barrier semaphores. Data moves between devices by JAX's collectives and lax.ppermute only.
A program may use at most 192 MiB of HBM per device.

```python
import math
import jax
import jax.numpy as jnp
from jax import lax

VARS = 8
CH = 64
HID = 256
STENCIL = 9
TAPS_IN = 4
TILE_ROWS = 16
TILE_WIDTH = 256
LL_DEV = 16384
TILE = 4096
CELLS = 524288
LL = 2097152
CAP = 512
TILE_COLS = 16
PAD = 4644
N_CELLS = 128


def count_table(key, salt):
    counts = jax.random.randint(jax.random.fold_in(key, salt), (N_CELLS, N_CELLS), max(1, CAP // 3), CAP + 1)
    return counts.at[N_CELLS - 1, :].set(CAP)


def slot_draw(key, salt, points, per_device):
    counts = count_table(key, salt)
    owner = jnp.arange(points, dtype=jnp.int32) // per_device
    first = jax.random.randint(jax.random.fold_in(key, salt + 100), (1, points), 0, N_CELLS)
    step_up = (jnp.arange(TAPS_IN, dtype=jnp.int32) // 2)[:, None]
    source = (first + step_up) % N_CELLS
    limit = counts[source, owner[None, :]]
    within = jax.random.randint(jax.random.fold_in(key, salt + 200), (TAPS_IN, points), 0, limit)
    table = source * CAP + within
    table = table.at[0, ::per_device].set(N_CELLS * CAP - 1)
    table = table.at[1, ::per_device].set(0)
    return table.astype(jnp.int32)


def draw_in_rows(key, part):
    table = jax.random.randint(jax.random.fold_in(key, 11), (N_CELLS, N_CELLS, CAP), 0, LL_DEV)
    return table.at[0, 0, 0].set(LL_DEV - 1).at[0, 0, 1].set(0).astype(jnp.int32)


def draw_out_rows(key, part):
    table = jax.random.randint(jax.random.fold_in(key, 12), (N_CELLS, N_CELLS, CAP), 0, TILE)
    return table.at[0, 0, 0].set(TILE - 1).at[0, 0, 1].set(0).astype(jnp.int32)


def draw_in_slot(key, part):
    return slot_draw(key, 1, N_CELLS * TILE, TILE)


def draw_out_slot(key, part):
    return slot_draw(key, 2, N_CELLS * LL_DEV, LL_DEV)


def draw_neighbours(key, part):
    points = N_CELLS * TILE
    global_cell = jnp.arange(points, dtype=jnp.int32)
    cell = global_cell % TILE
    row_pos = cell // TILE_WIDTH
    col_pos = cell % TILE_WIDTH
    direction = jnp.arange(STENCIL, dtype=jnp.int32)[:, None]
    table = (row_pos + 1 + direction // 3 - 1) * (TILE_WIDTH + 2) + col_pos + 1 + direction % 3 - 1
    row_edge = (row_pos == 0) | (row_pos == TILE_ROWS - 1)
    col_edge = (col_pos == 0) | (col_pos == TILE_WIDTH - 1)
    chosen = jax.random.randint(jax.random.fold_in(key, 31), (points,), 0, 2) == 1
    chosen = chosen & row_edge & col_edge & (global_cell >= TILE)
    row_step = jnp.where(row_pos == 0, -1, 1)
    col_step = jnp.where(col_pos == 0, -1, 1)
    diagonal = (row_step + 1) * 3 + col_step + 1
    replaced = (row_pos + 1 + row_step) * (TILE_WIDTH + 2) + col_pos + 1
    hit = chosen[None, :] & (direction == diagonal[None, :])
    return jnp.where(hit, replaced[None, :], table).astype(jnp.int32)


def levels(key, dims, pieces, least, top_value):
    gain = 1.0
    for position, parts in pieces:
        steps = jax.random.uniform(jax.random.fold_in(jax.random.fold_in(key, 6), position), (parts,), jnp.float32, least / len(pieces), top_value / len(pieces))
        gain = gain * jnp.repeat(jnp.exp(steps), dims[position] // parts).reshape((-1,) + (1,) * (len(dims) - 1 - position))
    return gain


def centred(rng, extent, deviation, most, split=(), held_as=jnp.bfloat16):
    gain = levels(rng, extent, split, -0.22, 0.18) if split else 1.0
    entries = jax.random.normal(rng, extent, jnp.float32) * deviation * gain
    return jnp.minimum(jnp.maximum(entries, -most), most).astype(held_as)


def setup_inputs(seed: int = 0) -> dict:
    key_list = jax.random.split(jax.random.key(seed), 14)
    return {
        "ll_fields": centred(key_list[0], (VARS, LL), 1.0, 6.0, ((1, 128),)),
        "target": centred(key_list[1], (VARS, LL), 1.0, 6.0, ((1, 128),)),
        "in_rows": draw_in_rows(jax.random.fold_in(key_list[13], 71), 0),
        "in_slot": draw_in_slot(jax.random.fold_in(key_list[13], 71), 0),
        "in_weight": jnp.clip(0.1 + 0.5 * jax.random.uniform(key_list[4], (TAPS_IN, CELLS), jnp.float32) ** levels(key_list[4], (TAPS_IN, CELLS), ((1, 128),), -0.2, 0.2), 0.1, 0.6),
        "neighbours": draw_neighbours(jax.random.fold_in(key_list[13], 71), 0),
        "conv_weight": centred(key_list[6], (CH, VARS * STENCIL), (VARS * STENCIL) ** -0.5, 0.75),
        "up_weight": centred(key_list[7], (HID, CH), CH ** -0.5, 0.75),
        "down_weight": centred(key_list[8], (CH, HID), HID ** -0.5, 0.375),
        "head_weight": centred(key_list[9], (VARS, CH), CH ** -0.5, 0.75),
        "out_rows": draw_out_rows(jax.random.fold_in(key_list[13], 71), 0),
        "out_slot": draw_out_slot(jax.random.fold_in(key_list[13], 71), 0),
        "out_weight": jnp.clip(0.1 + 0.5 * jax.random.uniform(key_list[12], (TAPS_IN, LL), jnp.float32) ** levels(key_list[12], (TAPS_IN, LL), ((1, 128),), -0.2, 0.2), 0.1, 0.6),
    }


def spread_taps(flattened, slot_table, weight_table):
    running = jnp.zeros((flattened.shape[0], slot_table.shape[1]), jnp.float32)
    for tap_index in range(slot_table.shape[0]):
        running = running + weight_table[tap_index] * flattened[:, slot_table[tap_index]].astype(jnp.float32)
    return running

def outer_sum(first_side, second_side):
    return lax.dot_general(first_side, second_side, (((1,), (1,)), ((), ())), preferred_element_type=jnp.float32)

def tile_forward(padded_flat, neighbour_table, conv_weight, up_weight, down_weight, head_weight):
    stacked = padded_flat[:, neighbour_table].reshape(-1, neighbour_table.shape[1])
    conv_out = jnp.dot(conv_weight, stacked, preferred_element_type=jnp.float32)
    conv_bf = conv_out.astype(jnp.bfloat16)
    pre_act = jnp.dot(up_weight, conv_bf, preferred_element_type=jnp.float32)
    activated = jax.nn.gelu(pre_act).astype(jnp.bfloat16)
    mixed_bf = (conv_out + jnp.dot(down_weight, activated, preferred_element_type=jnp.float32)).astype(jnp.bfloat16)
    head_out = jnp.dot(head_weight, mixed_bf, preferred_element_type=jnp.float32).astype(jnp.bfloat16)
    return (stacked, conv_bf, pre_act, activated, mixed_bf, head_out)

def tile_backward(saved, grad_out, up_weight, down_weight, head_weight):
    stacked, conv_bf, pre_act, activated, mixed_bf, head_out = saved
    grad_mixed = jnp.dot(head_weight.T, grad_out, preferred_element_type=jnp.float32)
    grad_mixed_bf = grad_mixed.astype(jnp.bfloat16)
    grad_head = outer_sum(grad_out, mixed_bf)
    grad_act = jnp.dot(down_weight.T, grad_mixed_bf, preferred_element_type=jnp.float32)
    grad_pre = jax.vjp(jax.nn.gelu, pre_act)[1](grad_act)[0].astype(jnp.bfloat16)
    grad_down = outer_sum(grad_mixed_bf, activated)
    grad_up = outer_sum(grad_pre, conv_bf)
    grad_conv_out = (grad_mixed + jnp.dot(up_weight.T, grad_pre, preferred_element_type=jnp.float32)).astype(jnp.bfloat16)
    grad_conv = outer_sum(grad_conv_out, stacked)
    return (grad_conv, grad_up, grad_down, grad_head)

def with_rims(regridded, tile_cols):
    left_col = jnp.roll(regridded[:, :, :, -1], 1, axis=0)
    right_col = jnp.roll(regridded[:, :, :, 0], -1, axis=0)
    middle = jnp.concatenate([left_col[..., None], regridded, right_col[..., None]], axis=3)
    top_row = jnp.roll(middle[:, :, -1, :], tile_cols, axis=0)
    bottom = jnp.roll(middle[:, :, 0, :], -tile_cols, axis=0)
    return jnp.concatenate([top_row[:, :, None], middle, bottom[:, :, None]], axis=2)

def reference(ll_fields, target, in_rows, in_slot, in_weight, neighbours, conv_weight, up_weight, down_weight, head_weight, out_rows, out_slot, out_weight):
    devices = N_CELLS
    device_ids = jnp.arange(devices, dtype=jnp.int32)
    band_base = (device_ids * LL_DEV)[:, None]
    tile_base = (device_ids * TILE)[:, None]

    def regrid_in(device):
        row_table = (in_rows[:, device, :] + band_base).reshape(-1)
        received = ll_fields[:, row_table]
        slot_table = lax.dynamic_slice_in_dim(in_slot, device * TILE, TILE, 1)
        weight_table = lax.dynamic_slice_in_dim(in_weight, device * TILE, TILE, 1)
        return spread_taps(received, slot_table, weight_table).astype(jnp.bfloat16).reshape(VARS, TILE_ROWS, TILE_WIDTH)
    regridded = lax.map(regrid_in, device_ids)
    padded = with_rims(regridded, TILE_COLS).reshape(devices, VARS, PAD)

    def tile_table(device):
        return lax.dynamic_slice_in_dim(neighbours, device * TILE, TILE, 1)

    def forward_one(device):
        return tile_forward(padded[device], tile_table(device), conv_weight, up_weight, down_weight, head_weight)[5]
    head_all = lax.map(forward_one, device_ids)
    head_flat = jnp.transpose(head_all, (1, 0, 2)).reshape(VARS, devices * TILE)
    loss_scale = 1.0 / math.sqrt(LL_DEV * devices)

    def regrid_out(band):
        row_table = (out_rows[:, band, :] + tile_base).reshape(-1)
        received = head_flat[:, row_table]
        slot_table = lax.dynamic_slice_in_dim(out_slot, band * LL_DEV, LL_DEV, 1)
        weight_table = lax.dynamic_slice_in_dim(out_weight, band * LL_DEV, LL_DEV, 1)
        band_pred = spread_taps(received, slot_table, weight_table).astype(jnp.bfloat16)
        band_target = lax.dynamic_slice_in_dim(target, band * LL_DEV, LL_DEV, 1)
        grad_pred = (band_pred.astype(jnp.float32) - band_target.astype(jnp.float32)) * loss_scale
        slot_grad = jnp.zeros((VARS, devices * CAP), jnp.float32)
        for tap_index in range(TAPS_IN):
            slot_grad = slot_grad.at[:, slot_table[tap_index]].add(weight_table[tap_index] * grad_pred)
        return (band_pred, slot_grad.astype(jnp.bfloat16).reshape(VARS, devices, CAP))
    pred_all, slot_grads = lax.map(regrid_out, device_ids)
    predicted = jnp.transpose(pred_all, (1, 0, 2)).reshape(VARS, LL_DEV * devices)

    def backward_one(carry, device):
        arriving = jnp.transpose(slot_grads[:, :, device, :], (1, 0, 2)).reshape(VARS, -1)
        row_table = out_rows[device].reshape(-1)
        grad_out = jnp.zeros((VARS, TILE), jnp.float32).at[:, row_table].add(arriving.astype(jnp.float32)).astype(jnp.bfloat16)
        saved = tile_forward(padded[device], tile_table(device), conv_weight, up_weight, down_weight, head_weight)
        terms = tile_backward(saved, grad_out, up_weight, down_weight, head_weight)
        return (tuple((running + term for running, term in zip(carry, terms))), None)
    start = (jnp.zeros((CH, VARS * STENCIL), jnp.float32), jnp.zeros((HID, CH), jnp.float32), jnp.zeros((CH, HID), jnp.float32), jnp.zeros((VARS, CH), jnp.float32))
    totals, _ = lax.scan(backward_one, start, device_ids)
    return (predicted, totals[0], totals[1], totals[2], totals[3])
```

```python
import functools, math
import jax, jax.numpy as jnp
from jax import lax
from jax.sharding import PartitionSpec as P
from jax.experimental import pallas as pl
from jax.experimental.pallas import tpu as pltpu
BF=jnp.bfloat16; F32=jnp.float32; I16=jnp.int16; I32=jnp.int32

def onehot(h, n):
    it = lax.broadcasted_iota(I16, (n, h.shape[1]), 0)
    hh = jnp.broadcast_to(h.astype(I16), (n, h.shape[1]))
    return jnp.where(it == hh, jnp.ones((), BF), jnp.zeros((), BF))

def pick(mm, lo, base, count, acc):
    l8 = jnp.broadcast_to(lo, (8, lo.shape[1]))
    for k in range(count):
        acc = jnp.where(l8 == base + k, mm[8*k:8*k+8], acc)
    return acc

def k4_body(BP, tab_ref, tgt_ref, slot_ref, w_ref, pred_ref, send_ref, oh_ref, e_ref, acc_ref):
    i = pl.program_id(0)
    scale = 1.0 / math.sqrt(2097152)
    def tap(t, p):
        idx = slot_ref[pl.ds(t,1), :]
        oh = onehot(idx & 511, 512)
        oh_ref[t] = oh
        d = idx >> 9
        def rows(r, a):
            mm = jnp.dot(tab_ref[pl.ds(pl.multiple_of(r*256,256), 256), :], oh, preferred_element_type=F32)
            return pick(mm, d - r*32, 0, 32, a)
        a = lax.fori_loop(0, 4, rows, jnp.zeros((8, BP), F32))
        return p + w_ref[pl.ds(t,1), :] * a
    p = lax.fori_loop(0, 4, tap, jnp.zeros((8, BP), F32))
    pb = p.astype(BF)
    pred_ref[...] = pb
    g = (pb.astype(F32) - tgt_ref[...].astype(F32)) * scale
    @pl.when(i == 0)
    def _(): acc_ref[...] = jnp.zeros_like(acc_ref)
    half = lax.broadcasted_iota(I16, (16, BP), 0) >> 3
    def back(t, c):
        idx = slot_ref[pl.ds(t,1), :]
        d = idx >> 9
        val = (w_ref[pl.ds(t,1), :] * g).astype(BF)
        val2 = jnp.concatenate([val, val], axis=0)
        q = jnp.broadcast_to(d.astype(I16), (16, BP)) - half
        z = jnp.zeros((), BF)
        for k in range(64):
            e_ref[16*k:16*k+16, :] = jnp.where(q == jnp.int16(2*k), val2, z)
        acc_ref[...] += lax.dot_general(e_ref[...], oh_ref[t], (((1,), (1,)), ((), ())), preferred_element_type=F32)
        return c
    lax.fori_loop(0, 4, back, 0)
    @pl.when(i == pl.num_programs(0)-1)
    def _(): send_ref[...] = acc_ref[...].astype(BF)

def k4(tab, target, slot, w, BP=512):
    points = target.shape[1]
    return pl.pallas_call(
        functools.partial(k4_body, BP),
        grid=(points//BP,),
        in_specs=[pl.BlockSpec((1024,512), lambda i:(0,0)), pl.BlockSpec((8,BP), lambda i:(0,i)),
                  pl.BlockSpec((4,BP), lambda i:(0,i)), pl.BlockSpec((4,BP), lambda i:(0,i))],
        out_specs=[pl.BlockSpec((8,BP), lambda i:(0,i)), pl.BlockSpec((1024,512), lambda i:(0,0))],
        out_shape=[jax.ShapeDtypeStruct((8,points), BF), jax.ShapeDtypeStruct((1024,512), BF)],
        scratch_shapes=[pltpu.VMEM((4,512,BP), BF), pltpu.VMEM((1024,BP), BF), pltpu.VMEM((1024,512), F32)],
        name="k4",
    )(tab, target, slot, w)

def k1_body(ll_ref, rows_ref, out_ref, tab_ref):
    @pl.when(pl.program_id(0) == 0)
    def _():
        for k in range(32):
            a = ll_ref[:, 512*k:512*k+256]; b = ll_ref[:, 512*k+256:512*k+512]
            tab_ref[16*k:16*k+16, :] = jnp.concatenate([a, b], axis=0)
    def pair(j, c):
        outs = []
        for u in range(2):
            idx = rows_ref[pl.ds(2*j+u, 1), :]
            oh = onehot(idx & 255, 256)
            lo = idx >> 8
            def rr(r, a):
                mm = jnp.dot(tab_ref[pl.ds(pl.multiple_of(r*256,256), 256), :], oh, preferred_element_type=F32)
                return pick(mm, lo - r*32, 0, 32, a)
            outs.append(lax.fori_loop(0, 2, rr, jnp.zeros((8, 512), F32)))
        out_ref[pl.ds(pl.multiple_of(16*j,16),16), :] = jnp.concatenate(outs, 0).astype(BF)
        return c
    lax.fori_loop(0, 4, pair, 0)

def k1(ll, rows):
    return pl.pallas_call(k1_body, grid=(16,),
        in_specs=[pl.BlockSpec((8,16384), lambda i:(0,0)), pl.BlockSpec((8,512), lambda i:(i,0))],
        out_specs=pl.BlockSpec((64,512), lambda i:(i,0)),
        out_shape=jax.ShapeDtypeStruct((1024,512), BF),
        scratch_shapes=[pltpu.VMEM((512,256), BF)], name="k1")(ll, rows)

def k2_body(tab_ref, slot_ref, w_ref, out_ref):
    def tap(t, p):
        idx = slot_ref[pl.ds(t,1), :]
        oh = onehot(idx & 511, 512)
        d = idx >> 9
        def rows(r, a):
            mm = jnp.dot(tab_ref[pl.ds(pl.multiple_of(r*256,256), 256), :], oh, preferred_element_type=F32)
            return pick(mm, d - r*32, 0, 32, a)
        a = lax.fori_loop(0, 4, rows, jnp.zeros((8, 512), F32))
        return p + w_ref[pl.ds(t,1), :] * a
    p = lax.fori_loop(0, 4, tap, jnp.zeros((8, 512), F32))
    out_ref[...] = p.astype(BF)

def k2(tab, slot, w):
    return pl.pallas_call(k2_body, grid=(8,),
        in_specs=[pl.BlockSpec((1024,512), lambda i:(0,0)), pl.BlockSpec((4,512), lambda i:(0,i)), pl.BlockSpec((4,512), lambda i:(0,i))],
        out_specs=pl.BlockSpec((8,512), lambda i:(0,i)),
        out_shape=jax.ShapeDtypeStruct((8,4096), BF), name="k2")(tab, slot, w)

def k3_body(ho_ref, rows_ref, out_ref, tab_ref):
    @pl.when(pl.program_id(0) == 0)
    def _():
        for k in range(8):
            a = ho_ref[:, 512*k:512*k+256]; b = ho_ref[:, 512*k+256:512*k+512]
            tab_ref[16*k:16*k+16, :] = jnp.concatenate([a, b], axis=0)
    def pair(j, c):
        outs = []
        for u in range(2):
            idx = rows_ref[pl.ds(2*j+u, 1), :]
            oh = onehot(idx & 255, 256)
            mm = jnp.dot(tab_ref[...], oh, preferred_element_type=F32)
            outs.append(pick(mm, idx >> 8, 0, 16, jnp.zeros((8,512), F32)))
        out_ref[pl.ds(pl.multiple_of(16*j,16),16), :] = jnp.concatenate(outs, 0).astype(BF)
        return c
    lax.fori_loop(0, 4, pair, 0)

def k3(ho, rows):
    return pl.pallas_call(k3_body, grid=(16,),
        in_specs=[pl.BlockSpec((8,4096), lambda i:(0,0)), pl.BlockSpec((8,512), lambda i:(i,0))],
        out_specs=pl.BlockSpec((64,512), lambda i:(i,0)),
        out_shape=jax.ShapeDtypeStruct((1024,512), BF),
        scratch_shapes=[pltpu.VMEM((128,256), BF)], name="k3")(ho, rows)

def k5_body(sg_ref, rows_ref, out_ref, e_ref, oh_ref, acc_ref):
    i = pl.program_id(0)
    @pl.when(i == 0)
    def _(): acc_ref[...] = jnp.zeros_like(acc_ref)
    half = lax.broadcasted_iota(I16, (16, 512), 0) >> 3
    z = jnp.zeros((), BF)
    for j in range(4):
        v2 = sg_ref[16*j:16*j+16, :]
        for u in range(2):
            val = v2[8*u:8*u+8]
            val2 = jnp.concatenate([val, val], 0)
            idx = rows_ref[2*j+u:2*j+u+1, :]
            n0 = (2*j+u)*512
            oh_ref[:, n0:n0+512] = onehot(idx & 255, 256)
            q = jnp.broadcast_to((idx >> 8).astype(I16), (16, 512)) - half
            for k in range(8):
                e_ref[16*k:16*k+16, n0:n0+512] = jnp.where(q == jnp.int16(2*k), val2, z)
    acc_ref[...] += lax.dot_general(e_ref[...], oh_ref[...], (((1,), (1,)), ((), ())), preferred_element_type=F32)
    @pl.when(i == pl.num_programs(0)-1)
    def _():
        for k in range(16):
            out_ref[:, 256*k:256*k+256] = acc_ref[8*k:8*k+8, :].astype(BF)

def k5(sg, rows):
    return pl.pallas_call(k5_body, grid=(16,),
        in_specs=[pl.BlockSpec((64,512), lambda i:(i,0)), pl.BlockSpec((8,512), lambda i:(i,0))],
        out_specs=pl.BlockSpec((8,4096), lambda i:(0,0)),
        out_shape=jax.ShapeDtypeStruct((8,4096), BF),
        scratch_shapes=[pltpu.VMEM((128,4096), BF), pltpu.VMEM((256,4096), BF), pltpu.VMEM((128,256), F32)], name="k5")(sg, rows)


VARS = 8
GRID_ROWS = 8
TILE_ROWS = 16
TILE_WIDTH = 256

def from_behind(value, axis, by):
    devices = lax.axis_size(axis)
    return lax.ppermute(value, axis, [(i, (i + by) % devices) for i in range(devices)])


def outer_sum(first_side, second_side):
    return lax.dot_general(
        first_side, second_side, (((1,), (1,)), ((), ())), preferred_element_type=jnp.float32
    )


def stencil_stack(padded, neighbours):
    row_count = padded.shape[1] - 2
    col_count = padded.shape[2] - 2
    pieces = [
        padded[
            :,
            direction // 3 : direction // 3 + row_count,
            direction % 3 : direction % 3 + col_count,
        ].reshape(padded.shape[0], row_count * col_count)
        for direction in range(9)
    ]
    stacked = jnp.stack(pieces, axis=1)
    corner_cells = jnp.array(
        [0, col_count - 1, (row_count - 1) * col_count, row_count * col_count - 1], jnp.int32
    )
    flat_padded = padded.reshape(padded.shape[0], -1)
    corner_values = flat_padded[:, neighbours[:, corner_cells]]
    stacked = stacked.at[:, :, corner_cells].set(corner_values)
    return stacked.reshape(-1, row_count * col_count)


def tile_forward(stacked, conv_weight, up_weight, down_weight, head_weight):
    conv_out = jnp.dot(conv_weight, stacked, preferred_element_type=jnp.float32)
    conv_bf = conv_out.astype(jnp.bfloat16)
    pre_act = jnp.dot(up_weight, conv_bf, preferred_element_type=jnp.float32)
    activated = jax.nn.gelu(pre_act).astype(jnp.bfloat16)
    mixed_bf = (
        conv_out + jnp.dot(down_weight, activated, preferred_element_type=jnp.float32)
    ).astype(jnp.bfloat16)
    head_out = jnp.dot(head_weight, mixed_bf, preferred_element_type=jnp.float32).astype(
        jnp.bfloat16
    )
    return (stacked, conv_bf, pre_act, activated, mixed_bf, head_out)


def tile_backward(saved, grad_out, up_weight, down_weight, head_weight):
    stacked, conv_bf, pre_act, activated, mixed_bf, head_out = saved
    grad_mixed = jnp.dot(head_weight.T, grad_out, preferred_element_type=jnp.float32)
    grad_mixed_bf = grad_mixed.astype(jnp.bfloat16)
    grad_head = outer_sum(grad_out, mixed_bf)
    grad_act = jnp.dot(down_weight.T, grad_mixed_bf, preferred_element_type=jnp.float32)
    grad_pre = jax.vjp(jax.nn.gelu, pre_act)[1](grad_act)[0].astype(jnp.bfloat16)
    grad_down = outer_sum(grad_mixed_bf, activated)
    grad_up = outer_sum(grad_pre, conv_bf)
    grad_conv_out = (
        grad_mixed + jnp.dot(up_weight.T, grad_pre, preferred_element_type=jnp.float32)
    ).astype(jnp.bfloat16)
    grad_conv = outer_sum(grad_conv_out, stacked)
    return (grad_conv, grad_up, grad_down, grad_head)


def column_from(piece_part, offset):
    return from_behind(piece_part, "cells", offset)


def row_from(piece_part, offset):
    return from_behind(piece_part, "cells", offset)


def body(
    ll_fields, target, in_rows, in_slot, in_weight, neighbours, conv_weight, up_weight, down_weight,
    head_weight, out_rows, out_slot, out_weight,
):
    devices = lax.axis_size("cells")
    tile_cols = devices // GRID_ROWS
    exchange = functools.partial(
        lax.all_to_all, axis_name="cells", split_axis=0, concat_axis=0, tiled=True
    )
    received = exchange(k1(ll_fields, in_rows[0]))
    regridded = k2(received, in_slot, in_weight)
    regridded = regridded.reshape(VARS, TILE_ROWS, TILE_WIDTH)
    left_col = column_from(regridded[:, :, TILE_WIDTH - 1], 1)
    right_col = column_from(regridded[:, :, 0], -1)
    middle = jnp.concatenate([left_col[:, :, None], regridded, right_col[:, :, None]], axis=2)
    upper_line = row_from(middle[:, TILE_ROWS - 1, :], tile_cols)
    lower_line = row_from(middle[:, 0, :], -tile_cols)
    padded = jnp.concatenate([upper_line[:, None, :], middle, lower_line[:, None, :]], axis=1)
    stacked = stencil_stack(padded, neighbours)
    saved = tile_forward(stacked, conv_weight, up_weight, down_weight, head_weight)
    head_out = saved[5]
    arrived = exchange(k3(head_out, out_rows[0]))
    predicted, slot_grad = k4(arrived, target, out_slot, out_weight)
    returned = exchange(slot_grad)
    grad_out = k5(returned, out_rows[0])
    terms = tile_backward(saved, grad_out, up_weight, down_weight, head_weight)
    flat = jnp.concatenate([term.reshape(-1) for term in terms]).reshape(devices, -1)
    part = jnp.sum(exchange(flat), axis=0, keepdims=True)
    whole = exchange(jnp.broadcast_to(part, flat.shape)).reshape(-1)
    totals, at = [], 0
    for term in terms:
        totals.append(whole[at : at + term.size].reshape(term.shape))
        at += term.size
    return (predicted, *totals)


def solution(mesh):
    placed = (
        P(None, "cells"),
        P(None, "cells"),
        P("cells", None, None),
        P(None, "cells"),
        P(None, "cells"),
        P(None, "cells"),
        P(),
        P(),
        P(),
        P(),
        P("cells", None, None),
        P(None, "cells"),
        P(None, "cells"),
    )
    return jax.shard_map(
        body,
        mesh=mesh,
        in_specs=placed,
        out_specs=(P(None, "cells"), P(), P(), P(), P()),
        check_vma=False,
    )
```

```python
import functools
import math

import jax
import jax.numpy as jnp
from jax import lax
from jax.experimental import pallas as pl
from jax.experimental.pallas import tpu as pltpu
from jax.sharding import PartitionSpec as P

BF = jnp.bfloat16
F32 = jnp.float32
I16 = jnp.int16
I32 = jnp.int32
VARS = 8
GRID_ROWS = 8
TILE_ROWS = 16
TILE_WIDTH = 256

def onehot(h, n):
    it = lax.broadcasted_iota(I16, (n, h.shape[1]), 0)
    hh = jnp.broadcast_to(h.astype(I16), (n, h.shape[1]))
    return jnp.where(it == hh, jnp.ones((), BF), jnp.zeros((), BF))

def picktree(mm, lo, count):
    l8 = jnp.broadcast_to(lo, (8, lo.shape[1]))
    masks = {}
    c = count // 2
    while c:
        masks[c] = (l8 & c) != 0
        c //= 2
    def tree(base, n):
        if n == 1: return mm[8*base:8*base+8]
        h = n // 2
        a = tree(base, h); b = tree(base+h, h)
        return jnp.where(masks[h], b, a)
    return tree(0, count)

def k4d_body(BP, tab_ref, tgt_ref, slot_ref, w_ref, pred_ref, send_ref, oh_ref, acc_ref):
    i = pl.program_id(0)
    scale = 1.0 / math.sqrt(2097152)
    @pl.when(i == 0)
    def _(): acc_ref[...] = jnp.zeros_like(acc_ref)
    p = jnp.zeros((8, BP), F32)
    for t in range(4):
        idx = slot_ref[t:t+1, :]
        oh = onehot(idx & 511, 512)
        oh_ref[:, t*BP:(t+1)*BP] = oh
        mm = jnp.dot(tab_ref[...], oh, preferred_element_type=F32)
        p = p + w_ref[t:t+1, :] * picktree(mm, idx >> 9, 128)
    pb = p.astype(BF)
    pred_ref[...] = pb
    g = (pb.astype(F32) - tgt_ref[...].astype(F32)) * scale
    half = lax.broadcasted_iota(I16, (16, 4*BP), 0) >> 3
    z = jnp.zeros((), BF)
    val = jnp.concatenate([(w_ref[t:t+1, :] * g).astype(BF) for t in range(4)], axis=1)
    d = jnp.concatenate([slot_ref[t:t+1, :] >> 9 for t in range(4)], axis=1)
    val2 = jnp.concatenate([val, val], axis=0)
    q = jnp.broadcast_to(d.astype(I16), (16, 4*BP)) - half
    e = jnp.concatenate([jnp.where(q == jnp.int16(2*k), val2, z) for k in range(64)], axis=0)
    acc_ref[...] += lax.dot_general(e, oh_ref[...], (((1,), (1,)), ((), ())), preferred_element_type=F32)
    @pl.when(i == pl.num_programs(0)-1)
    def _(): send_ref[...] = acc_ref[...].astype(BF)

def k2c_body(BC, tab_ref, slot_ref, w_ref, out_ref):
    p = jnp.zeros((8, BC), F32)
    for t in range(4):
        idx = slot_ref[t:t+1, :]
        mm = jnp.dot(tab_ref[...], onehot(idx & 511, 512), preferred_element_type=F32)
        p = p + w_ref[t:t+1, :] * picktree(mm, idx >> 9, 128)
    out_ref[...] = p.astype(BF)

def k2c(tab, slot, w, BC=512):
    return pl.pallas_call(functools.partial(k2c_body, BC), grid=(4096//BC,),
        in_specs=[pl.BlockSpec((1024,512), lambda i:(0,0)), pl.BlockSpec((4,BC), lambda i:(0,i)), pl.BlockSpec((4,BC), lambda i:(0,i))],
        out_specs=pl.BlockSpec((8,BC), lambda i:(0,i)),
        out_shape=jax.ShapeDtypeStruct((8,4096), BF), name="k2")(tab, slot, w)

def k1c_body(ll_ref, rows_ref, out_ref, tab_ref):
    @pl.when(pl.program_id(0) == 0)
    def _():
        for k in range(16):
            a = ll_ref[:, 1024*k:1024*k+512]; b = ll_ref[:, 1024*k+512:1024*k+1024]
            tab_ref[16*k:16*k+16, :] = jnp.concatenate([a, b], axis=0)
    for j in range(4):
        outs = []
        for u in range(2):
            idx = rows_ref[2*j+u:2*j+u+1, :]
            mm = jnp.dot(tab_ref[...], onehot(idx & 511, 512), preferred_element_type=F32)
            outs.append(picktree(mm, idx >> 9, 32))
        out_ref[16*j:16*j+16, :] = jnp.concatenate(outs, 0).astype(BF)

def k1c(ll, rows):
    return pl.pallas_call(k1c_body, grid=(16,),
        in_specs=[pl.BlockSpec((8,16384), lambda i:(0,0)), pl.BlockSpec((8,512), lambda i:(i,0))],
        out_specs=pl.BlockSpec((64,512), lambda i:(i,0)),
        out_shape=jax.ShapeDtypeStruct((1024,512), BF),
        scratch_shapes=[pltpu.VMEM((256,512), BF)], name="k1")(ll, rows)

def mk4(body, ohs, BP):
    def k4(tab, target, slot, w):
        points = target.shape[1]
        return pl.pallas_call(
            functools.partial(body, BP),
            grid=(points//BP,),
            in_specs=[pl.BlockSpec((1024,512), lambda i:(0,0)), pl.BlockSpec((8,BP), lambda i:(0,i)),
                      pl.BlockSpec((4,BP), lambda i:(0,i)), pl.BlockSpec((4,BP), lambda i:(0,i))],
            out_specs=[pl.BlockSpec((8,BP), lambda i:(0,i)), pl.BlockSpec((1024,512), lambda i:(0,0))],
            out_shape=[jax.ShapeDtypeStruct((8,points), BF), jax.ShapeDtypeStruct((1024,512), BF)],
            scratch_shapes=[pltpu.VMEM(ohs, BF), pltpu.VMEM((1024,512), F32)],
            name="k4",
        )(tab, target, slot, w)
    return k4

def kf_body(reg_ref, lc_ref, rc_ref, up_ref, lw_ref, n0_ref, n1_ref, n2_ref, n3_ref, cw_ref, uw_ref, dw_ref, hw_ref, rows_ref,
            out_ref, st_ref, tab_ref):
    @pl.when(pl.program_id(0) == 0)
    def _():
        w = 256
        reg = reg_ref[...].astype(F32)
        pick_col = (lax.broadcasted_iota(I32, (16, 4096), 1) == 256 * lax.broadcasted_iota(I32, (16, 4096), 0))
        spread = jnp.where(pick_col, 1.0, 0.0).astype(BF)
        lcol = jnp.dot(lc_ref[...], spread, preferred_element_type=F32)
        rcol = pltpu.roll(jnp.dot(rc_ref[...], spread, preferred_element_type=F32), 255, 1)
        col = lax.broadcasted_iota(I32, (8, 4096), 1) & 255
        left = jnp.where(col == 0, lcol, pltpu.roll(reg, 1, 1))
        right = jnp.where(col == 255, rcol, pltpu.roll(reg, 4095, 1))
        def line(ref, swap_l, swap_r):
            x = ref[...].astype(F32)
            a, b, c = x[:, 0:w], x[:, 1:w+1], x[:, 2:w+2]
            lane = lax.broadcasted_iota(I32, (8, w), 1)
            a = jnp.where((lane == 0) & swap_l, b, a)
            c = jnp.where((lane == w-1) & swap_r, b, c)
            return a, b, c
        ups = line(up_ref, n0_ref[0:1, 0:1] != 0, n1_ref[2:3, 127:128] != 257)
        lows = line(lw_ref, n2_ref[6:7, 0:1] != 17*258, n3_ref[8:9, 127:128] != 17*258+257)
        for dc, mid in enumerate((left, reg, right)):
            full = jnp.concatenate([ups[dc], mid, lows[dc]], axis=1).astype(BF)
            for dr in range(3):
                st_ref[(dr*3+dc)*8:(dr*3+dc)*8+8, :] = full[:, dr*w:dr*w+4096]
        def chunk(j, c):
            s = st_ref[:, pl.ds(pl.multiple_of(j*512, 512), 512)]
            conv = jnp.dot(cw_ref[...], s, preferred_element_type=F32)
            pre = jnp.dot(uw_ref[...], conv.astype(BF), preferred_element_type=F32)
            act = jax.nn.gelu(pre).astype(BF)
            mixed = (conv + jnp.dot(dw_ref[...], act, preferred_element_type=F32)).astype(BF)
            head = jnp.dot(hw_ref[...], mixed, preferred_element_type=F32).astype(BF)
            tab_ref[pl.ds(pl.multiple_of(16*j,16),16), :] = jnp.concatenate([head[:, :256], head[:, 256:]], axis=0)
            return c
        lax.fori_loop(0, 8, chunk, 0)
    for j in range(8):
        outs = []
        for u in range(2):
            idx = rows_ref[2*j+u:2*j+u+1, :]
            mm = jnp.dot(tab_ref[...], onehot(idx & 255, 256), preferred_element_type=F32)
            outs.append(picktree(mm, idx >> 8, 16))
        out_ref[16*j:16*j+16, :] = jnp.concatenate(outs, 0).astype(BF)

def kf(reg, lc, rc, up, lw, neigh, cw, uw, dw, hw, rows):
    fix = lambda s: pl.BlockSpec(s, lambda i: (0, 0))
    nb = lambda b: pl.BlockSpec((9, 128), lambda i: (0, b))
    return pl.pallas_call(kf_body, grid=(8,),
        in_specs=[fix((8,4096)), fix((8,16)), fix((8,16)), fix((8,258)), fix((8,258)), nb(0), nb(1), nb(30), nb(31),
                  fix((64,72)), fix((256,64)), fix((64,256)), fix((8,64)), pl.BlockSpec((16,512), lambda i:(i,0))],
        out_specs=[pl.BlockSpec((128,512), lambda i:(i,0)), fix((72,4096))],
        out_shape=[jax.ShapeDtypeStruct((1024,512), BF), jax.ShapeDtypeStruct((72,4096), BF)],
        scratch_shapes=[pltpu.VMEM((128,256), BF)], name="kf",
    )(reg, lc, rc, up, lw, neigh, neigh, neigh, neigh, cw, uw, dw, hw, rows)

def gelu_both(x):
    c = math.sqrt(2 / math.pi)
    x2 = x * x
    th = jnp.tanh(c * (x + 0.044715 * x2 * x))
    act = x * (0.5 * (1.0 + th))
    der = 0.5 * (1.0 + th) + 0.5 * x * (1.0 - th * th) * (c * (1.0 + 3 * 0.044715 * x2))
    return act, der

def nt(a, b):
    return lax.dot_general(a, b, (((1,), (1,)), ((), ())), preferred_element_type=F32)

def kb_body(sg_ref, rows_ref, st_ref, cw_ref, uw_ref, dw_ref, hw_ref, ut_ref, dt_ref, ht_ref,
            gc_ref, gu_ref, gd_ref, gh_ref, acc_ref):
    i = pl.program_id(0)
    @pl.when(i == 0)
    def _(): acc_ref[...] = jnp.zeros_like(acc_ref)
    half = lax.broadcasted_iota(I16, (16, 4096), 0) >> 3
    z = jnp.zeros((), BF)
    val = jnp.concatenate([sg_ref[8*j:8*j+8, :] for j in range(8)], axis=1)
    idx = jnp.concatenate([rows_ref[j:j+1, :] for j in range(8)], axis=1)
    val2 = jnp.concatenate([val, val], axis=0)
    q = jnp.broadcast_to((idx >> 8).astype(I16), (16, 4096)) - half
    e = jnp.concatenate([jnp.where(q == jnp.int16(2*k), val2, z) for k in range(8)], axis=0)
    acc_ref[...] += nt(e, onehot(idx & 255, 256))
    @pl.when(i == pl.num_programs(0)-1)
    def _():
        gc_ref[...] = jnp.zeros_like(gc_ref); gu_ref[...] = jnp.zeros_like(gu_ref)
        gd_ref[...] = jnp.zeros_like(gd_ref); gh_ref[...] = jnp.zeros_like(gh_ref)
        def chunk(j, c):
            s = st_ref[:, pl.ds(pl.multiple_of(j*512, 512), 512)]
            a2 = acc_ref[pl.ds(pl.multiple_of(16*j,16),16), :]
            go = jnp.concatenate([a2[:8], a2[8:]], axis=1).astype(BF)
            conv = jnp.dot(cw_ref[...], s, preferred_element_type=F32)
            cb = conv.astype(BF)
            pre = jnp.dot(uw_ref[...], cb, preferred_element_type=F32)
            act, der = gelu_both(pre)
            act = act.astype(BF)
            mixed = (conv + jnp.dot(dw_ref[...], act, preferred_element_type=F32)).astype(BF)
            gm = jnp.dot(ht_ref[...], go, preferred_element_type=F32)
            gmb = gm.astype(BF)
            gh_ref[...] += nt(go, mixed)
            gp = (jnp.dot(dt_ref[...], gmb, preferred_element_type=F32) * der).astype(BF)
            gd_ref[...] += nt(gmb, act)
            gu_ref[...] += nt(gp, cb)
            gco = (gm + jnp.dot(ut_ref[...], gp, preferred_element_type=F32)).astype(BF)
            gc_ref[...] += nt(gco, s)
            return c
        lax.fori_loop(0, 8, chunk, 0)

def kb(sg, rows, st, cw, uw, dw, hw):
    fix = lambda s: pl.BlockSpec(s, lambda i: (0, 0))
    return pl.pallas_call(kb_body, grid=(16,),
        in_specs=[pl.BlockSpec((64,512), lambda i:(i,0)), pl.BlockSpec((8,512), lambda i:(i,0)), fix((72,4096)),
                  fix((64,72)), fix((256,64)), fix((64,256)), fix((8,64)), fix((64,256)), fix((256,64)), fix((64,8))],
        out_specs=[fix((64,72)), fix((256,64)), fix((64,256)), fix((8,64))],
        out_shape=[jax.ShapeDtypeStruct(s, F32) for s in ((64,72), (256,64), (64,256), (8,64))],
        scratch_shapes=[pltpu.VMEM((128,256), F32)], name="kb",
    )(sg, rows, st, cw, uw, dw, hw, uw.T, dw.T, hw.T)

k4d = mk4(k4d_body, (512, 2048), 512)


def from_behind(value, by):
    devices = lax.axis_size("cells")
    return lax.ppermute(value, "cells", [(i, (i + by) % devices) for i in range(devices)])


def body(
    ll_fields, target, in_rows, in_slot, in_weight, neighbours, conv_weight, up_weight, down_weight,
    head_weight, out_rows, out_slot, out_weight,
):
    devices = lax.axis_size("cells")
    tile_cols = devices // GRID_ROWS
    exchange = functools.partial(
        lax.all_to_all, axis_name="cells", split_axis=0, concat_axis=0, tiled=True
    )
    received = exchange(k1c(ll_fields, in_rows[0]))
    flat_reg = k2c(received, in_slot, in_weight)
    regridded = flat_reg.reshape(VARS, TILE_ROWS, TILE_WIDTH)
    left_col = from_behind(regridded[:, :, TILE_WIDTH - 1], 1)
    right_col = from_behind(regridded[:, :, 0], -1)
    last, first = TILE_ROWS - 1, 0
    line = lambda r: jnp.concatenate(
        [left_col[:, r : r + 1], regridded[:, r, :], right_col[:, r : r + 1]], axis=1
    )
    upper_line = from_behind(line(last), tile_cols)
    lower_line = from_behind(line(first), -tile_cols)
    conv_w = conv_weight.reshape(64, VARS, 9).transpose(0, 2, 1).reshape(64, 72)
    sending, stacked = kf(
        flat_reg, left_col, right_col, upper_line, lower_line, neighbours, conv_w, up_weight,
        down_weight, head_weight, out_rows[0],
    )
    arrived = exchange(sending)
    predicted, slot_grad = k4d(arrived, target, out_slot, out_weight)
    returned = exchange(slot_grad)
    terms = kb(returned, out_rows[0], stacked, conv_w, up_weight, down_weight, head_weight)
    flat = jnp.concatenate([term.reshape(-1) for term in terms]).reshape(devices, -1)
    part = jnp.sum(exchange(flat), axis=0, keepdims=True)
    whole = exchange(jnp.broadcast_to(part, flat.shape)).reshape(-1)
    totals, at = [], 0
    for term in terms:
        totals.append(whole[at : at + term.size].reshape(term.shape))
        at += term.size
    totals[0] = totals[0].reshape(64, 9, VARS).transpose(0, 2, 1).reshape(64, 72)
    return (predicted, *totals)


def solution(mesh):
    placed = (
        P(None, "cells"),
        P(None, "cells"),
        P("cells", None, None),
        P(None, "cells"),
        P(None, "cells"),
        P(None, "cells"),
        P(),
        P(),
        P(),
        P(),
        P("cells", None, None),
        P(None, "cells"),
        P(None, "cells"),
    )
    return jax.shard_map(
        body,
        mesh=mesh,
        in_specs=placed,
        out_specs=(P(None, "cells"), P(), P(), P(), P()),
        check_vma=False,
    )
```

```python
import functools
import math

import jax
import jax.numpy as jnp
from jax import lax
from jax.experimental import pallas as pl
from jax.experimental.pallas import tpu as pltpu
from jax.sharding import PartitionSpec as P

BF = jnp.bfloat16
F32 = jnp.float32
I16 = jnp.int16
I32 = jnp.int32
VARS = 8
GRID_ROWS = 8
TILE_ROWS = 16
TILE_WIDTH = 256

def onehot(h, n):
    it = lax.broadcasted_iota(I16, (n, h.shape[1]), 0)
    hh = jnp.broadcast_to(h.astype(I16), (n, h.shape[1]))
    return jnp.where(it == hh, jnp.ones((), BF), jnp.zeros((), BF))

def picktree(mm, lo, count):
    l8 = jnp.broadcast_to(lo, (8, lo.shape[1]))
    masks = {}
    c = count // 2
    while c:
        masks[c] = (l8 & c) != 0
        c //= 2
    def tree(base, n):
        if n == 1: return mm[8*base:8*base+8]
        h = n // 2
        a = tree(base, h); b = tree(base+h, h)
        return jnp.where(masks[h], b, a)
    return tree(0, count)

def k1c_body(ll_ref, rows_ref, out_ref, tab_ref):
    @pl.when(pl.program_id(0) == 0)
    def _():
        for k in range(16):
            a = ll_ref[:, 1024*k:1024*k+512]; b = ll_ref[:, 1024*k+512:1024*k+1024]
            tab_ref[16*k:16*k+16, :] = jnp.concatenate([a, b], axis=0)
    for j in range(4):
        outs = []
        for u in range(2):
            idx = rows_ref[2*j+u:2*j+u+1, :]
            mm = jnp.dot(tab_ref[...], onehot(idx & 511, 512), preferred_element_type=F32)
            outs.append(picktree(mm, idx >> 9, 32))
        out_ref[16*j:16*j+16, :] = jnp.concatenate(outs, 0).astype(BF)

def k1c(ll, rows):
    return pl.pallas_call(k1c_body, grid=(16,),
        in_specs=[pl.BlockSpec((8,16384), lambda i:(0,0)), pl.BlockSpec((8,512), lambda i:(i,0))],
        out_specs=pl.BlockSpec((64,512), lambda i:(i,0)),
        out_shape=jax.ShapeDtypeStruct((1024,512), BF),
        scratch_shapes=[pltpu.VMEM((256,512), BF)], name="k1")(ll, rows)

def kf_body(reg_ref, lc_ref, rc_ref, up_ref, lw_ref, n0_ref, n1_ref, n2_ref, n3_ref, cw_ref, uw_ref, dw_ref, hw_ref, rows_ref,
            out_ref, st_ref, tab_ref):
    @pl.when(pl.program_id(0) == 0)
    def _():
        w = 256
        reg = reg_ref[...].astype(F32)
        pick_col = (lax.broadcasted_iota(I32, (16, 4096), 1) == 256 * lax.broadcasted_iota(I32, (16, 4096), 0))
        spread = jnp.where(pick_col, 1.0, 0.0).astype(BF)
        lcol = jnp.dot(lc_ref[...], spread, preferred_element_type=F32)
        rcol = pltpu.roll(jnp.dot(rc_ref[...], spread, preferred_element_type=F32), 255, 1)
        col = lax.broadcasted_iota(I32, (8, 4096), 1) & 255
        left = jnp.where(col == 0, lcol, pltpu.roll(reg, 1, 1))
        right = jnp.where(col == 255, rcol, pltpu.roll(reg, 4095, 1))
        def line(ref, swap_l, swap_r):
            x = ref[...].astype(F32)
            a, b, c = x[:, 0:w], x[:, 1:w+1], x[:, 2:w+2]
            lane = lax.broadcasted_iota(I32, (8, w), 1)
            a = jnp.where((lane == 0) & swap_l, b, a)
            c = jnp.where((lane == w-1) & swap_r, b, c)
            return a, b, c
        ups = line(up_ref, n0_ref[0:1, 0:1] != 0, n1_ref[2:3, 127:128] != 257)
        lows = line(lw_ref, n2_ref[6:7, 0:1] != 17*258, n3_ref[8:9, 127:128] != 17*258+257)
        for dc, mid in enumerate((left, reg, right)):
            full = jnp.concatenate([ups[dc], mid, lows[dc]], axis=1).astype(BF)
            for dr in range(3):
                st_ref[(dr*3+dc)*8:(dr*3+dc)*8+8, :] = full[:, dr*w:dr*w+4096]
        def chunk(j, c):
            s = st_ref[:, pl.ds(pl.multiple_of(j*512, 512), 512)]
            conv = jnp.dot(cw_ref[...], s, preferred_element_type=F32)
            pre = jnp.dot(uw_ref[...], conv.astype(BF), preferred_element_type=F32)
            act = jax.nn.gelu(pre).astype(BF)
            mixed = (conv + jnp.dot(dw_ref[...], act, preferred_element_type=F32)).astype(BF)
            head = jnp.dot(hw_ref[...], mixed, preferred_element_type=F32).astype(BF)
            tab_ref[pl.ds(pl.multiple_of(16*j,16),16), :] = jnp.concatenate([head[:, :256], head[:, 256:]], axis=0)
            return c
        lax.fori_loop(0, 8, chunk, 0)
    for j in range(8):
        outs = []
        for u in range(2):
            idx = rows_ref[2*j+u:2*j+u+1, :]
            mm = jnp.dot(tab_ref[...], onehot(idx & 255, 256), preferred_element_type=F32)
            outs.append(picktree(mm, idx >> 8, 16))
        out_ref[16*j:16*j+16, :] = jnp.concatenate(outs, 0).astype(BF)

def kf(reg, lc, rc, up, lw, neigh, cw, uw, dw, hw, rows):
    fix = lambda s: pl.BlockSpec(s, lambda i: (0, 0))
    nb = lambda b: pl.BlockSpec((9, 128), lambda i: (0, b))
    return pl.pallas_call(kf_body, grid=(8,),
        in_specs=[fix((8,4096)), fix((8,16)), fix((8,16)), fix((8,258)), fix((8,258)), nb(0), nb(1), nb(30), nb(31),
                  fix((64,72)), fix((256,64)), fix((64,256)), fix((8,64)), pl.BlockSpec((16,512), lambda i:(i,0))],
        out_specs=[pl.BlockSpec((128,512), lambda i:(i,0)), fix((72,4096))],
        out_shape=[jax.ShapeDtypeStruct((1024,512), BF), jax.ShapeDtypeStruct((72,4096), BF)],
        scratch_shapes=[pltpu.VMEM((128,256), BF)], name="kf",
    )(reg, lc, rc, up, lw, neigh, neigh, neigh, neigh, cw, uw, dw, hw, rows)

def gelu_both(x):
    c = math.sqrt(2 / math.pi)
    x2 = x * x
    th = jnp.tanh(c * (x + 0.044715 * x2 * x))
    act = x * (0.5 * (1.0 + th))
    der = 0.5 * (1.0 + th) + 0.5 * x * (1.0 - th * th) * (c * (1.0 + 3 * 0.044715 * x2))
    return act, der

def nt(a, b):
    return lax.dot_general(a, b, (((1,), (1,)), ((), ())), preferred_element_type=F32)

def kb_body(sg_ref, rows_ref, st_ref, cw_ref, uw_ref, dw_ref, hw_ref, ut_ref, dt_ref, ht_ref,
            gc_ref, gu_ref, gd_ref, gh_ref, acc_ref):
    i = pl.program_id(0)
    @pl.when(i == 0)
    def _(): acc_ref[...] = jnp.zeros_like(acc_ref)
    half = lax.broadcasted_iota(I16, (16, 4096), 0) >> 3
    z = jnp.zeros((), BF)
    val = jnp.concatenate([sg_ref[8*j:8*j+8, :] for j in range(8)], axis=1)
    idx = jnp.concatenate([rows_ref[j:j+1, :] for j in range(8)], axis=1)
    val2 = jnp.concatenate([val, val], axis=0)
    q = jnp.broadcast_to((idx >> 8).astype(I16), (16, 4096)) - half
    e = jnp.concatenate([jnp.where(q == jnp.int16(2*k), val2, z) for k in range(8)], axis=0)
    acc_ref[...] += nt(e, onehot(idx & 255, 256))
    @pl.when(i == pl.num_programs(0)-1)
    def _():
        gc_ref[...] = jnp.zeros_like(gc_ref); gu_ref[...] = jnp.zeros_like(gu_ref)
        gd_ref[...] = jnp.zeros_like(gd_ref); gh_ref[...] = jnp.zeros_like(gh_ref)
        def chunk(j, c):
            s = st_ref[:, pl.ds(pl.multiple_of(j*512, 512), 512)]
            a2 = acc_ref[pl.ds(pl.multiple_of(16*j,16),16), :]
            go = jnp.concatenate([a2[:8], a2[8:]], axis=1).astype(BF)
            conv = jnp.dot(cw_ref[...], s, preferred_element_type=F32)
            cb = conv.astype(BF)
            pre = jnp.dot(uw_ref[...], cb, preferred_element_type=F32)
            act, der = gelu_both(pre)
            act = act.astype(BF)
            mixed = (conv + jnp.dot(dw_ref[...], act, preferred_element_type=F32)).astype(BF)
            gm = jnp.dot(ht_ref[...], go, preferred_element_type=F32)
            gmb = gm.astype(BF)
            gh_ref[...] += nt(go, mixed)
            gp = (jnp.dot(dt_ref[...], gmb, preferred_element_type=F32) * der).astype(BF)
            gd_ref[...] += nt(gmb, act)
            gu_ref[...] += nt(gp, cb)
            gco = (gm + jnp.dot(ut_ref[...], gp, preferred_element_type=F32)).astype(BF)
            gc_ref[...] += nt(gco, s)
            return c
        lax.fori_loop(0, 8, chunk, 0)

def kb(sg, rows, st, cw, uw, dw, hw):
    fix = lambda s: pl.BlockSpec(s, lambda i: (0, 0))
    return pl.pallas_call(kb_body, grid=(16,),
        in_specs=[pl.BlockSpec((64,512), lambda i:(i,0)), pl.BlockSpec((8,512), lambda i:(i,0)), fix((72,4096)),
                  fix((64,72)), fix((256,64)), fix((64,256)), fix((8,64)), fix((64,256)), fix((256,64)), fix((64,8))],
        out_specs=[fix((64,72)), fix((256,64)), fix((64,256)), fix((8,64))],
        out_shape=[jax.ShapeDtypeStruct(s, F32) for s in ((64,72), (256,64), (64,256), (8,64))],
        scratch_shapes=[pltpu.VMEM((128,256), F32)], name="kb",
    )(sg, rows, st, cw, uw, dw, hw, uw.T, dw.T, hw.T)

def prep_body(slot_ref, pos_ref, code_ref, gid_ref, ohp_ref):
    idx = jnp.concatenate([slot_ref[t:t+1, :] for t in range(4)], axis=1)
    d = idx >> 9
    g = d >> 4
    it8 = lax.broadcasted_iota(I32, (8, 256), 0)
    hot = [jnp.where(it8 == g[:, 256*b:256*b+256], 1.0, 0.0) for b in range(16)]
    a = jnp.concatenate(hot, axis=0).astype(BF)
    sq = lambda f, n: jnp.where(f(lax.broadcasted_iota(I32, (n, n), 0), lax.broadcasted_iota(I32, (n, n), 1)), 1.0, 0.0).astype(BF)
    excl = jnp.dot(a, sq(lambda r, c: r < c, 256), preferred_element_type=F32)
    tot = jnp.dot(a, jnp.ones((256, 256), BF), preferred_element_type=F32)
    prefix = jnp.dot(sq(lambda r, c: ((r & 7) == (c & 7)) & (c < (r & ~7)), 128), tot.astype(BF), preferred_element_type=F32)
    count = prefix[120:128] + tot[120:128]
    nblk = ((count.astype(I32) + 255) >> 8).astype(F32)
    both = jnp.concatenate([nblk, jnp.zeros_like(nblk)], axis=0).astype(BF)
    base = jnp.dot(sq(lambda r, c: c < r, 16), both, preferred_element_type=F32)[:8]
    lane = lax.broadcasted_iota(I32, (8, 256), 1).astype(F32)
    gid = jnp.sum(jnp.where(lane >= base + nblk, 1.0, 0.0), axis=0, keepdims=True).astype(I32)
    gid_ref[0] = jnp.minimum(gid, 7)
    first = 256.0 * base
    pos = jnp.concatenate([
        jnp.sum(hot[b] * (excl[8*b:8*b+8] + prefix[8*b:8*b+8] + first), axis=0, keepdims=True) for b in range(16)
    ], axis=1).astype(I32)
    pos_ref[0] = pos
    ohp_ref[...] = onehot(pos & 255, 256)
    z = jnp.zeros((), BF)
    q = jnp.broadcast_to((pos >> 8).astype(I16), (16, 4096)) - lax.broadcasted_iota(I16, (16, 4096), 0)
    low = jnp.broadcast_to((idx & 255).astype(F32), (16, 4096)).astype(BF)
    high = jnp.broadcast_to(((idx >> 8) & 31).astype(F32), (16, 4096)).astype(BF)
    e = jnp.concatenate([jnp.where(q == jnp.int16(16*k), v, z) for v in (low, high) for k in range(2)], axis=0)
    r = nt(e, ohp_ref[...])
    code_ref[...] = (r[:32] + 256.0 * r[32:]).astype(I32)

def prep(slot):
    n = slot.shape[1] // 1024
    return pl.pallas_call(prep_body, grid=(n,),
        in_specs=[pl.BlockSpec((4,1024), lambda i:(0,i))],
        out_specs=[pl.BlockSpec((1,1,4096), lambda i:(i,0,0)), pl.BlockSpec((32,256), lambda i:(i,0)), pl.BlockSpec((1,1,256), lambda i:(i,0,0))],
        out_shape=[jax.ShapeDtypeStruct((n,1,4096), I32), jax.ShapeDtypeStruct((32*n,256), I32), jax.ShapeDtypeStruct((n,1,256), I32)],
        scratch_shapes=[pltpu.VMEM((256,4096), BF)], name="prep",
        cost_estimate=pl.CostEstimate(flops=n*1600000000, bytes_accessed=n*60000, transcendentals=0),
    )(slot)

def tree24(mm, blk):
    l8 = jnp.broadcast_to(blk, (8, blk.shape[1]))
    m = {c: (l8 & c) != 0 for c in (1, 2, 4, 8, 16)}
    def tree(base, n):
        if n == 1: return mm[8*base:8*base+8]
        h = n // 2
        return jnp.where(m[h], tree(base+h, h), tree(base, h)) if n < 32 else jnp.where(m[16], tree(16, 8), tree(0, 16))
    return tree(0, 32)

def look_up(i, tab_ref, code_ref, gid_ref, res_ref, oh_ref):
    for b in range(0, NB, 2):
        outs = []
        for u in range(2):
            code = code_ref[b+u:b+u+1, :]
            oh = onehot(code & 511, 512)
            if oh_ref is not None:
                oh_ref[:, 256*(b+u):256*(b+u+1)] = oh
            rows = tab_ref[pl.ds(pl.multiple_of(gid_ref[i, b+u] * 128, 128), 128), :]
            mm = jnp.dot(rows, oh, preferred_element_type=F32)
            outs.append(picktree(mm, code >> 9, 16))
        res_ref[8*b:8*b+16, :] = jnp.concatenate(outs, axis=0).astype(BF)

def blend(pos_ref, w_ref, res_ref, ohp_ref, n):
    p = jnp.zeros((8, n), F32)
    for t in range(4):
        pos = pos_ref[0, :, t*n:(t+1)*n]
        ohp = onehot(pos & 255, 256)
        if ohp_ref is not None:
            ohp_ref[:, t*n:(t+1)*n] = ohp
        mm = jnp.dot(res_ref[...], ohp, preferred_element_type=F32)
        p = p + w_ref[t:t+1, :] * tree24(mm, pos >> 8)
    return p

def k4s_body(gid_ref, tab_ref, tgt_ref, w_ref, pos_ref, code_ref, pred_ref, send_ref, res_ref, oh_ref, ohp_ref, acc_ref):
    i = pl.program_id(0)
    n = 1024
    scale = 1.0 / math.sqrt(2097152)
    @pl.when(i == 0)
    def _(): acc_ref[...] = jnp.zeros_like(acc_ref)
    look_up(i, tab_ref, code_ref, gid_ref, res_ref, oh_ref)
    pb = blend(pos_ref, w_ref, res_ref, ohp_ref, n).astype(BF)
    pred_ref[...] = pb
    g = (pb.astype(F32) - tgt_ref[...].astype(F32)) * scale
    z = jnp.zeros((), BF)
    val = jnp.concatenate([(w_ref[t:t+1, :] * g).astype(BF) for t in range(4)], axis=1)
    val2 = jnp.concatenate([val, val], axis=0)
    half = lax.broadcasted_iota(I16, (16, 4*n), 0) >> 3
    q = jnp.broadcast_to((pos_ref[0] >> 8).astype(I16), (16, 4*n)) - half
    e = jnp.concatenate([jnp.where(q == jnp.int16(2*k), val2, z) for k in range(NB//2)], axis=0)
    sv = nt(e, ohp_ref[...]).astype(BF)
    half = lax.broadcasted_iota(I16, (16, 256), 0) >> 3
    for b in range(NB):
        vb = sv[8*b:8*b+8]
        v2 = jnp.concatenate([vb, vb], axis=0)
        q = jnp.broadcast_to((code_ref[b:b+1, :] >> 9).astype(I16), (16, 256)) - half
        eb = jnp.concatenate([jnp.where(q == jnp.int16(2*k), v2, z) for k in range(8)], axis=0)
        at = pl.ds(pl.multiple_of(gid_ref[i, b] * 128, 128), 128)
        acc_ref[at, :] += nt(eb, oh_ref[:, 256*b:256*b+256])
    @pl.when(i == pl.num_programs(0)-1)
    def _(): send_ref[...] = acc_ref[...].astype(BF)

def k4s_main(tab, target, w, pos, code, gid):
    points = target.shape[1]
    return pl.pallas_call(k4s_body, grid=(points//1024,),
        in_specs=[pl.BlockSpec(memory_space=pltpu.SMEM), pl.BlockSpec((1024,512), lambda i:(0,0)), pl.BlockSpec((8,1024), lambda i:(0,i)),
                  pl.BlockSpec((4,1024), lambda i:(0,i)), pl.BlockSpec((1,1,4096), lambda i:(i,0,0)), pl.BlockSpec((32,256), lambda i:(i,0))],
        out_specs=[pl.BlockSpec((8,1024), lambda i:(0,i)), pl.BlockSpec((1024,512), lambda i:(0,0))],
        out_shape=[jax.ShapeDtypeStruct((8,points), BF), jax.ShapeDtypeStruct((1024,512), BF)],
        scratch_shapes=[pltpu.VMEM((8*NB,256), BF), pltpu.VMEM((512,256*NB), BF), pltpu.VMEM((256,4096), BF), pltpu.VMEM((1024,512), F32)],
        name="k4", compiler_params=pltpu.CompilerParams(vmem_limit_bytes=60*2**20),
    )(gid.reshape(-1, 256), tab, target, w, pos, code)

def k2s_body(gid_ref, tab_ref, w_ref, pos_ref, code_ref, out_ref, res_ref):
    look_up(pl.program_id(0), tab_ref, code_ref, gid_ref, res_ref, None)
    out_ref[...] = blend(pos_ref, w_ref, res_ref, None, 1024).astype(BF)

def k2s_main(tab, w, pos, code, gid):
    return pl.pallas_call(k2s_body, grid=(4,),
        in_specs=[pl.BlockSpec(memory_space=pltpu.SMEM), pl.BlockSpec((1024,512), lambda i:(0,0)), pl.BlockSpec((4,1024), lambda i:(0,i)),
                  pl.BlockSpec((1,1,4096), lambda i:(i,0,0)), pl.BlockSpec((32,256), lambda i:(i,0))],
        out_specs=pl.BlockSpec((8,1024), lambda i:(0,i)),
        out_shape=jax.ShapeDtypeStruct((8,4096), BF),
        scratch_shapes=[pltpu.VMEM((8*NB,256), BF)], name="k2",
    )(gid.reshape(-1, 256), tab, w, pos, code)


NB = 24


def from_behind(value, by):
    devices = lax.axis_size("cells")
    return lax.ppermute(value, "cells", [(i, (i + by) % devices) for i in range(devices)])


def body(
    ll_fields, target, in_rows, in_slot, in_weight, neighbours, conv_weight, up_weight, down_weight,
    head_weight, out_rows, out_slot, out_weight,
):
    devices = lax.axis_size("cells")
    tile_cols = devices // GRID_ROWS
    exchange = functools.partial(
        lax.all_to_all, axis_name="cells", split_axis=0, concat_axis=0, tiled=True
    )
    in_plan = prep(in_slot)
    out_plan = prep(out_slot)
    received = exchange(k1c(ll_fields, in_rows[0]))
    flat_reg = k2s_main(received, in_weight, *in_plan)
    regridded = flat_reg.reshape(VARS, TILE_ROWS, TILE_WIDTH)
    left_col = from_behind(regridded[:, :, TILE_WIDTH - 1], 1)
    right_col = from_behind(regridded[:, :, 0], -1)
    last, first = TILE_ROWS - 1, 0
    line = lambda r: jnp.concatenate(
        [left_col[:, r : r + 1], regridded[:, r, :], right_col[:, r : r + 1]], axis=1
    )
    upper_line = from_behind(line(last), tile_cols)
    lower_line = from_behind(line(first), -tile_cols)
    conv_w = conv_weight.reshape(64, VARS, 9).transpose(0, 2, 1).reshape(64, 72)
    sending, stacked = kf(
        flat_reg, left_col, right_col, upper_line, lower_line, neighbours, conv_w, up_weight,
        down_weight, head_weight, out_rows[0],
    )
    arrived = exchange(sending)
    predicted, slot_grad = k4s_main(arrived, target, out_weight, *out_plan)
    returned = exchange(slot_grad)
    terms = kb(returned, out_rows[0], stacked, conv_w, up_weight, down_weight, head_weight)
    flat = jnp.concatenate([term.reshape(-1) for term in terms]).reshape(devices, -1)
    part = jnp.sum(exchange(flat), axis=0, keepdims=True)
    whole = exchange(jnp.broadcast_to(part, flat.shape)).reshape(-1)
    totals, at = [], 0
    for term in terms:
        totals.append(whole[at : at + term.size].reshape(term.shape))
        at += term.size
    totals[0] = totals[0].reshape(64, 9, VARS).transpose(0, 2, 1).reshape(64, 72)
    return (predicted, *totals)


def solution(mesh):
    placed = (
        P(None, "cells"),
        P(None, "cells"),
        P("cells", None, None),
        P(None, "cells"),
        P(None, "cells"),
        P(None, "cells"),
        P(),
        P(),
        P(),
        P(),
        P("cells", None, None),
        P(None, "cells"),
        P(None, "cells"),
    )
    return jax.shard_map(
        body,
        mesh=mesh,
        in_specs=placed,
        out_specs=(P(None, "cells"), P(), P(), P(), P()),
        check_vma=False,
    )
```

```python
import functools
import math

import jax
import jax.numpy as jnp
from jax import lax
from jax.experimental import pallas as pl
from jax.experimental.pallas import tpu as pltpu
from jax.sharding import PartitionSpec as P

BF = jnp.bfloat16
F32 = jnp.float32
I16 = jnp.int16
I32 = jnp.int32
VARS = 8
GRID_ROWS = 8
TILE_ROWS = 16
TILE_WIDTH = 256

def onehot(h, n):
    it = lax.broadcasted_iota(I16, (n, h.shape[1]), 0)
    hh = jnp.broadcast_to(h.astype(I16), (n, h.shape[1]))
    return jnp.where(it == hh, jnp.ones((), BF), jnp.zeros((), BF))

def picktree(mm, lo, count):
    l8 = jnp.broadcast_to(lo, (8, lo.shape[1]))
    masks = {}
    c = count // 2
    while c:
        masks[c] = (l8 & c) != 0
        c //= 2
    def tree(base, n):
        if n == 1: return mm[8*base:8*base+8]
        h = n // 2
        a = tree(base, h); b = tree(base+h, h)
        return jnp.where(masks[h], b, a)
    return tree(0, count)

def k1c_body(ll_ref, rows_ref, out_ref, tab_ref):
    @pl.when(pl.program_id(0) == 0)
    def _():
        for k in range(16):
            a = ll_ref[:, 1024*k:1024*k+512]; b = ll_ref[:, 1024*k+512:1024*k+1024]
            tab_ref[16*k:16*k+16, :] = jnp.concatenate([a, b], axis=0)
    for j in range(4):
        outs = []
        for u in range(2):
            idx = rows_ref[2*j+u:2*j+u+1, :]
            mm = jnp.dot(tab_ref[...], onehot(idx & 511, 512), preferred_element_type=F32)
            outs.append(picktree(mm, idx >> 9, 32))
        out_ref[16*j:16*j+16, :] = jnp.concatenate(outs, 0).astype(BF)

def k1c(ll, rows):
    return pl.pallas_call(k1c_body, grid=(16,),
        in_specs=[pl.BlockSpec((8,16384), lambda i:(0,0)), pl.BlockSpec((8,512), lambda i:(i,0))],
        out_specs=pl.BlockSpec((64,512), lambda i:(i,0)),
        out_shape=jax.ShapeDtypeStruct((1024,512), BF),
        scratch_shapes=[pltpu.VMEM((256,512), BF)], name="k1")(ll, rows)

def kf_body(reg_ref, lc_ref, rc_ref, up_ref, lw_ref, n0_ref, n1_ref, n2_ref, n3_ref, cw_ref, uw_ref, dw_ref, hw_ref, rows_ref,
            out_ref, st_ref, tab_ref):
    @pl.when(pl.program_id(0) == 0)
    def _():
        w = 256
        reg = reg_ref[...].astype(F32)
        pick_col = (lax.broadcasted_iota(I32, (16, 4096), 1) == 256 * lax.broadcasted_iota(I32, (16, 4096), 0))
        spread = jnp.where(pick_col, 1.0, 0.0).astype(BF)
        lcol = jnp.dot(lc_ref[...], spread, preferred_element_type=F32)
        rcol = pltpu.roll(jnp.dot(rc_ref[...], spread, preferred_element_type=F32), 255, 1)
        col = lax.broadcasted_iota(I32, (8, 4096), 1) & 255
        left = jnp.where(col == 0, lcol, pltpu.roll(reg, 1, 1))
        right = jnp.where(col == 255, rcol, pltpu.roll(reg, 4095, 1))
        def line(ref, swap_l, swap_r):
            x = ref[...].astype(F32)
            a, b, c = x[:, 0:w], x[:, 1:w+1], x[:, 2:w+2]
            lane = lax.broadcasted_iota(I32, (8, w), 1)
            a = jnp.where((lane == 0) & swap_l, b, a)
            c = jnp.where((lane == w-1) & swap_r, b, c)
            return a, b, c
        ups = line(up_ref, n0_ref[0:1, 0:1] != 0, n1_ref[2:3, 127:128] != 257)
        lows = line(lw_ref, n2_ref[6:7, 0:1] != 17*258, n3_ref[8:9, 127:128] != 17*258+257)
        for dc, mid in enumerate((left, reg, right)):
            full = jnp.concatenate([ups[dc], mid, lows[dc]], axis=1).astype(BF)
            for dr in range(3):
                st_ref[(dr*3+dc)*8:(dr*3+dc)*8+8, :] = full[:, dr*w:dr*w+4096]
        def chunk(j, c):
            s = st_ref[:, pl.ds(pl.multiple_of(j*512, 512), 512)]
            conv = jnp.dot(cw_ref[...], s, preferred_element_type=F32)
            pre = jnp.dot(uw_ref[...], conv.astype(BF), preferred_element_type=F32)
            act = jax.nn.gelu(pre).astype(BF)
            mixed = (conv + jnp.dot(dw_ref[...], act, preferred_element_type=F32)).astype(BF)
            head = jnp.dot(hw_ref[...], mixed, preferred_element_type=F32).astype(BF)
            tab_ref[pl.ds(pl.multiple_of(16*j,16),16), :] = jnp.concatenate([head[:, :256], head[:, 256:]], axis=0)
            return c
        lax.fori_loop(0, 8, chunk, 0)
    for j in range(8):
        outs = []
        for u in range(2):
            idx = rows_ref[2*j+u:2*j+u+1, :]
            mm = jnp.dot(tab_ref[...], onehot(idx & 255, 256), preferred_element_type=F32)
            outs.append(picktree(mm, idx >> 8, 16))
        out_ref[16*j:16*j+16, :] = jnp.concatenate(outs, 0).astype(BF)

def kf(reg, lc, rc, up, lw, neigh, cw, uw, dw, hw, rows):
    fix = lambda s: pl.BlockSpec(s, lambda i: (0, 0))
    nb = lambda b: pl.BlockSpec((9, 128), lambda i: (0, b))
    return pl.pallas_call(kf_body, grid=(8,),
        in_specs=[fix((8,4096)), fix((8,16)), fix((8,16)), fix((8,258)), fix((8,258)), nb(0), nb(1), nb(30), nb(31),
                  fix((64,72)), fix((256,64)), fix((64,256)), fix((8,64)), pl.BlockSpec((16,512), lambda i:(i,0))],
        out_specs=[pl.BlockSpec((128,512), lambda i:(i,0)), fix((72,4096))],
        out_shape=[jax.ShapeDtypeStruct((1024,512), BF), jax.ShapeDtypeStruct((72,4096), BF)],
        scratch_shapes=[pltpu.VMEM((128,256), BF)], name="kf",
    )(reg, lc, rc, up, lw, neigh, neigh, neigh, neigh, cw, uw, dw, hw, rows)

def gelu_both(x):
    c = math.sqrt(2 / math.pi)
    x2 = x * x
    th = jnp.tanh(c * (x + 0.044715 * x2 * x))
    act = x * (0.5 * (1.0 + th))
    der = 0.5 * (1.0 + th) + 0.5 * x * (1.0 - th * th) * (c * (1.0 + 3 * 0.044715 * x2))
    return act, der

def nt(a, b):
    return lax.dot_general(a, b, (((1,), (1,)), ((), ())), preferred_element_type=F32)

def kb_body(sg_ref, rows_ref, st_ref, cw_ref, uw_ref, dw_ref, hw_ref, ut_ref, dt_ref, ht_ref,
            gc_ref, gu_ref, gd_ref, gh_ref, acc_ref):
    i = pl.program_id(0)
    @pl.when(i == 0)
    def _(): acc_ref[...] = jnp.zeros_like(acc_ref)
    half = lax.broadcasted_iota(I16, (16, 4096), 0) >> 3
    z = jnp.zeros((), BF)
    val = jnp.concatenate([sg_ref[8*j:8*j+8, :] for j in range(8)], axis=1)
    idx = jnp.concatenate([rows_ref[j:j+1, :] for j in range(8)], axis=1)
    val2 = jnp.concatenate([val, val], axis=0)
    q = jnp.broadcast_to((idx >> 8).astype(I16), (16, 4096)) - half
    e = jnp.concatenate([jnp.where(q == jnp.int16(2*k), val2, z) for k in range(8)], axis=0)
    acc_ref[...] += nt(e, onehot(idx & 255, 256))
    @pl.when(i == pl.num_programs(0)-1)
    def _():
        gc_ref[...] = jnp.zeros_like(gc_ref); gu_ref[...] = jnp.zeros_like(gu_ref)
        gd_ref[...] = jnp.zeros_like(gd_ref); gh_ref[...] = jnp.zeros_like(gh_ref)
        def chunk(j, c):
            s = st_ref[:, pl.ds(pl.multiple_of(j*512, 512), 512)]
            a2 = acc_ref[pl.ds(pl.multiple_of(16*j,16),16), :]
            go = jnp.concatenate([a2[:8], a2[8:]], axis=1).astype(BF)
            conv = jnp.dot(cw_ref[...], s, preferred_element_type=F32)
            cb = conv.astype(BF)
            pre = jnp.dot(uw_ref[...], cb, preferred_element_type=F32)
            act, der = gelu_both(pre)
            act = act.astype(BF)
            mixed = (conv + jnp.dot(dw_ref[...], act, preferred_element_type=F32)).astype(BF)
            gm = jnp.dot(ht_ref[...], go, preferred_element_type=F32)
            gmb = gm.astype(BF)
            gh_ref[...] += nt(go, mixed)
            gp = (jnp.dot(dt_ref[...], gmb, preferred_element_type=F32) * der).astype(BF)
            gd_ref[...] += nt(gmb, act)
            gu_ref[...] += nt(gp, cb)
            gco = (gm + jnp.dot(ut_ref[...], gp, preferred_element_type=F32)).astype(BF)
            gc_ref[...] += nt(gco, s)
            return c
        lax.fori_loop(0, 8, chunk, 0)

def kb(sg, rows, st, cw, uw, dw, hw):
    fix = lambda s: pl.BlockSpec(s, lambda i: (0, 0))
    return pl.pallas_call(kb_body, grid=(16,),
        in_specs=[pl.BlockSpec((64,512), lambda i:(i,0)), pl.BlockSpec((8,512), lambda i:(i,0)), fix((72,4096)),
                  fix((64,72)), fix((256,64)), fix((64,256)), fix((8,64)), fix((64,256)), fix((256,64)), fix((64,8))],
        out_specs=[fix((64,72)), fix((256,64)), fix((64,256)), fix((8,64))],
        out_shape=[jax.ShapeDtypeStruct(s, F32) for s in ((64,72), (256,64), (64,256), (8,64))],
        scratch_shapes=[pltpu.VMEM((128,256), F32)], name="kb",
    )(sg, rows, st, cw, uw, dw, hw, uw.T, dw.T, hw.T)

def prep_body(slot_ref, pos_ref, code_ref, gid_ref, ohp_ref):
    idx = jnp.concatenate([slot_ref[t:t+1, :] for t in range(4)], axis=1)
    d = idx >> 9
    g = (d * 147) >> 11
    it = lax.broadcasted_iota(I32, (16, 256), 0)
    hot = [jnp.where(it == g[:, 256*b:256*b+256], 1.0, 0.0) for b in range(16)]
    a = jnp.concatenate(hot, axis=0).astype(BF)
    sq = lambda f, n: jnp.where(f(lax.broadcasted_iota(I32, (n, n), 0), lax.broadcasted_iota(I32, (n, n), 1)), 1.0, 0.0).astype(BF)
    excl = jnp.dot(a, sq(lambda r, c: r < c, 256), preferred_element_type=F32)
    tot = jnp.dot(a, jnp.ones((256, 256), BF), preferred_element_type=F32)
    prefix = jnp.dot(sq(lambda r, c: ((r & 15) == (c & 15)) & (c < (r & ~15)), 256), tot.astype(BF), preferred_element_type=F32)
    count = prefix[240:256] + tot[240:256]
    nblk = ((count.astype(I32) + 255) >> 8).astype(F32)
    base = jnp.dot(sq(lambda r, c: c < r, 16), nblk.astype(BF), preferred_element_type=F32)
    lane = lax.broadcasted_iota(I32, (16, 256), 1)
    gid = jnp.sum(jnp.where(lane.astype(F32) >= base + nblk, 1.0, 0.0), axis=0, keepdims=True).astype(I32)
    used = jnp.sum(nblk, axis=0, keepdims=True).astype(I32)
    gid_ref[0] = jnp.where(lane[:1] == 255, used, jnp.minimum(gid, GROUPS - 1))
    first = 256.0 * base
    pos = jnp.concatenate([
        jnp.sum(hot[b] * (excl[16*b:16*b+16] + prefix[16*b:16*b+16] + first), axis=0, keepdims=True) for b in range(16)
    ], axis=1).astype(I32)
    pos_ref[0] = pos
    ohp_ref[...] = onehot(pos & 255, 256)
    z = jnp.zeros((), BF)
    q = jnp.broadcast_to((pos >> 8).astype(I16), (16, 4096)) - lax.broadcasted_iota(I16, (16, 4096), 0)
    code = (idx & 511) + ((d - SPAN * g) << 9)
    low = jnp.broadcast_to((code & 255).astype(F32), (16, 4096)).astype(BF)
    high = jnp.broadcast_to((code >> 8).astype(F32), (16, 4096)).astype(BF)
    e = jnp.concatenate([jnp.where(q == jnp.int16(16*k), v, z) for v in (low, high) for k in range(2)], axis=0)
    r = nt(e, ohp_ref[...])
    code_ref[...] = (r[:32] + 256.0 * r[32:]).astype(I32)

def prep(slot, start, n):
    return pl.pallas_call(prep_body, grid=(n,),
        in_specs=[pl.BlockSpec((4,1024), lambda i:(0,i+start))],
        out_specs=[pl.BlockSpec((1,1,4096), lambda i:(i,0,0)), pl.BlockSpec((32,256), lambda i:(i,0)), pl.BlockSpec((1,1,256), lambda i:(i,0,0))],
        out_shape=[jax.ShapeDtypeStruct((n,1,4096), I32), jax.ShapeDtypeStruct((32*n,256), I32), jax.ShapeDtypeStruct((n,1,256), I32)],
        scratch_shapes=[pltpu.VMEM((256,4096), BF)], name="prep",
        cost_estimate=pl.CostEstimate(flops=n*1600000000, bytes_accessed=n*60000, transcendentals=0),
    )(slot)

def tree_pick(mm, lo, count):
    l8 = jnp.broadcast_to(lo, (8, lo.shape[1]))
    top = 1
    while top < count: top *= 2
    m = {}
    h = top // 2
    while h:
        m[h] = (l8 & h) != 0
        h //= 2
    def tree(base, n):
        if n == 1: return mm[8*base:8*base+8]
        h = n // 2
        if base + h >= count: return tree(base, h)
        return jnp.where(m[h], tree(base+h, h), tree(base, h))
    return tree(0, top)

def load_table(tab_ref, nat_ref):
    nat_ref[:1024] = tab_ref[...]
    nat_ref[1024:] = jnp.zeros((8*SPAN*GROUPS-1024, 512), BF)

def look_up(i, nb, nat_ref, code_ref, gid_ref, res_ref, oh_ref):
    half = nb // 2
    def go(j, c):
        for h in range(0, half, 2):
            outs = []
            for u in range(2):
                b = j*half + h + u
                code = code_ref[pl.ds(b, 1), :]
                oh = onehot(code & 511, 512)
                if oh_ref is not None: oh_ref[b] = oh
                at = pl.ds(pl.multiple_of(gid_ref[i, b] * (8*SPAN), 16), 8*SPAN)
                outs.append(tree_pick(jnp.dot(nat_ref[at, :], oh, preferred_element_type=F32), code >> 9, SPAN))
            res_ref[pl.ds(pl.multiple_of(8*(j*half+h), 16), 16), :] = jnp.concatenate(outs, axis=0).astype(BF)
        return c
    lax.fori_loop(0, 2, go, 0)

def blend(nb, pos_ref, w_ref, res_ref, ohp_ref, n):
    p = jnp.zeros((8, n), F32)
    for t in range(4):
        pos = pos_ref[0, :, t*n:(t+1)*n]
        ohp = onehot(pos & 255, 256)
        if ohp_ref is not None:
            ohp_ref[:, t*n:(t+1)*n] = ohp
        mm = jnp.dot(res_ref[:8*nb, :], ohp, preferred_element_type=F32)
        p = p + w_ref[t:t+1, :] * tree_pick(mm, pos >> 8, nb)
    return p

def k4_body(gid_ref, tab_ref, tgt_ref, w_ref, pos_ref, code_ref, pred_ref, send_ref,
            res_ref, oh_ref, ohp_ref, sv_ref, nat_ref, acc0_ref, acc1_ref):
    i = pl.program_id(0)
    n = 1024
    scale = 1.0 / math.sqrt(2097152)
    @pl.when(i == 0)
    def _():
        load_table(tab_ref, nat_ref)
        acc0_ref[...] = jnp.zeros_like(acc0_ref)
        acc1_ref[...] = jnp.zeros_like(acc1_ref)
    def run(nb):
        look_up(i, nb, nat_ref, code_ref, gid_ref, res_ref, oh_ref)
        pb = blend(nb, pos_ref, w_ref, res_ref, ohp_ref, n).astype(BF)
        pred_ref[...] = pb
        g = (pb.astype(F32) - tgt_ref[...].astype(F32)) * scale
        z = jnp.zeros((), BF)
        val = jnp.concatenate([(w_ref[t:t+1, :] * g).astype(BF) for t in range(4)], axis=1)
        val2 = jnp.concatenate([val, val], axis=0)
        row = lax.broadcasted_iota(I16, (16, 4*n), 0) >> 3
        q = jnp.broadcast_to((pos_ref[0] >> 8).astype(I16), (16, 4*n)) - row
        e = jnp.concatenate([jnp.where(q == jnp.int16(2*k), val2, z) for k in range(nb//2)], axis=0)
        sv_ref[:8*nb, :] = nt(e, ohp_ref[...]).astype(BF)
        row = lax.broadcasted_iota(I16, (16, 256), 0) >> 3
        half = nb // 2
        def back(j, c):
            for h in range(0, half, 2):
                pair = sv_ref[pl.ds(pl.multiple_of(8*(j*half+h), 16), 16), :]
                for u, acc_ref in enumerate((acc0_ref, acc1_ref)):
                    b = j*half + h + u
                    vb = pair[8*u:8*u+8]
                    v2 = jnp.concatenate([vb, vb], axis=0)
                    q = jnp.broadcast_to((code_ref[pl.ds(b, 1), :] >> 9).astype(I16), (16, 256)) - row
                    eb = jnp.concatenate([jnp.where(q == jnp.int16(2*k), v2, z) for k in range(SPAN//2)], axis=0)
                    at = pl.ds(pl.multiple_of(gid_ref[i, b] * (8*SPAN), 16), 8*SPAN)
                    acc_ref[at, :] += nt(eb, oh_ref[b])
            return c
        lax.fori_loop(0, 2, back, 0)
    used = gid_ref[i, 255]
    @pl.when(used <= FEW)
    def _(): run(FEW)
    @pl.when(used > FEW)
    def _(): run(MANY)
    @pl.when(i == pl.num_programs(0)-1)
    def _(): send_ref[...] = (acc0_ref[:1024] + acc1_ref[:1024]).astype(BF)

def k4(tab, target, w, pos, code, gid):
    points = target.shape[1]
    rows = 8*SPAN*GROUPS
    return pl.pallas_call(k4_body, grid=(points//1024,),
        in_specs=[pl.BlockSpec(memory_space=pltpu.SMEM), pl.BlockSpec((1024,512), lambda i:(0,0)), pl.BlockSpec((8,1024), lambda i:(0,i)),
                  pl.BlockSpec((4,1024), lambda i:(0,i)), pl.BlockSpec((1,1,4096), lambda i:(i,0,0)), pl.BlockSpec((32,256), lambda i:(i,0))],
        out_specs=[pl.BlockSpec((8,1024), lambda i:(0,i)), pl.BlockSpec((1024,512), lambda i:(0,0))],
        out_shape=[jax.ShapeDtypeStruct((8,points), BF), jax.ShapeDtypeStruct((1024,512), BF)],
        scratch_shapes=[pltpu.VMEM((8*MANY,256), BF), pltpu.VMEM((MANY,512,256), BF), pltpu.VMEM((256,4096), BF), pltpu.VMEM((8*MANY,256), BF),
                        pltpu.VMEM((rows,512), BF), pltpu.VMEM((rows,512), F32), pltpu.VMEM((rows,512), F32)],
        name="k4", compiler_params=pltpu.CompilerParams(vmem_limit_bytes=60*2**20),
    )(gid.reshape(-1, 256), tab, target, w, pos, code)

def k2_body(gid_ref, tab_ref, w_ref, pos_ref, code_ref, out_ref, res_ref, nat_ref):
    i = pl.program_id(0)
    @pl.when(i == 0)
    def _(): load_table(tab_ref, nat_ref)
    def run(nb):
        look_up(i, nb, nat_ref, code_ref, gid_ref, res_ref, None)
        out_ref[...] = blend(nb, pos_ref, w_ref, res_ref, None, 1024).astype(BF)
    used = gid_ref[i, 255]
    @pl.when(used <= FEW)
    def _(): run(FEW)
    @pl.when(used > FEW)
    def _(): run(MANY)

def k2(tab, w, pos, code, gid):
    return pl.pallas_call(k2_body, grid=(4,),
        in_specs=[pl.BlockSpec(memory_space=pltpu.SMEM), pl.BlockSpec((1024,512), lambda i:(0,0)), pl.BlockSpec((4,1024), lambda i:(0,i)),
                  pl.BlockSpec((1,1,4096), lambda i:(i,0,0)), pl.BlockSpec((32,256), lambda i:(i,0))],
        out_specs=pl.BlockSpec((8,1024), lambda i:(0,i)),
        out_shape=jax.ShapeDtypeStruct((8,4096), BF),
        scratch_shapes=[pltpu.VMEM((8*MANY,256), BF), pltpu.VMEM((8*SPAN*GROUPS,512), BF)], name="k2",
    )(gid.reshape(-1, 256), tab, w, pos, code)


SPAN = 14
GROUPS = 10
FEW, MANY = 20, 28


def from_behind(value, by):
    devices = lax.axis_size("cells")
    return lax.ppermute(value, "cells", [(i, (i + by) % devices) for i in range(devices)])


def body(
    ll_fields, target, in_rows, in_slot, in_weight, neighbours, conv_weight, up_weight, down_weight,
    head_weight, out_rows, out_slot, out_weight,
):
    devices = lax.axis_size("cells")
    tile_cols = devices // GRID_ROWS
    exchange = functools.partial(
        lax.all_to_all, axis_name="cells", split_axis=0, concat_axis=0, tiled=True
    )
    in_plan = prep(in_slot, 0, 4)
    head_plan = prep(out_slot, 0, 7)
    received = exchange(k1c(ll_fields, in_rows[0]))
    received, head_plan = lax.optimization_barrier((received, head_plan))
    flat_reg = k2(received, in_weight, *in_plan)
    regridded = flat_reg.reshape(VARS, TILE_ROWS, TILE_WIDTH)
    left_col = from_behind(regridded[:, :, TILE_WIDTH - 1], 1)
    right_col = from_behind(regridded[:, :, 0], -1)
    last, first = TILE_ROWS - 1, 0
    line = lambda r: jnp.concatenate(
        [left_col[:, r : r + 1], regridded[:, r, :], right_col[:, r : r + 1]], axis=1
    )
    upper_line = from_behind(line(last), tile_cols)
    lower_line = from_behind(line(first), -tile_cols)
    conv_w = conv_weight.reshape(64, VARS, 9).transpose(0, 2, 1).reshape(64, 72)
    sending, stacked = kf(
        flat_reg, left_col, right_col, upper_line, lower_line, neighbours, conv_w, up_weight,
        down_weight, head_weight, out_rows[0],
    )
    arrived = exchange(sending)
    tail_plan = prep(out_slot, 7, 9)
    out_plan = [jnp.concatenate(pair, axis=0) for pair in zip(head_plan, tail_plan)]
    predicted, slot_grad = k4(arrived, target, out_weight, *out_plan)
    returned = exchange(slot_grad)
    terms = kb(returned, out_rows[0], stacked, conv_w, up_weight, down_weight, head_weight)
    flat = jnp.concatenate([term.reshape(-1) for term in terms]).reshape(devices, -1)
    part = jnp.sum(exchange(flat), axis=0, keepdims=True)
    whole = exchange(jnp.broadcast_to(part, flat.shape)).reshape(-1)
    totals, at = [], 0
    for term in terms:
        totals.append(whole[at : at + term.size].reshape(term.shape))
        at += term.size
    totals[0] = totals[0].reshape(64, 9, VARS).transpose(0, 2, 1).reshape(64, 72)
    return (predicted, *totals)


def solution(mesh):
    placed = (
        P(None, "cells"),
        P(None, "cells"),
        P("cells", None, None),
        P(None, "cells"),
        P(None, "cells"),
        P(None, "cells"),
        P(),
        P(),
        P(),
        P(),
        P("cells", None, None),
        P(None, "cells"),
        P(None, "cells"),
    )
    return jax.shard_map(
        body,
        mesh=mesh,
        in_specs=placed,
        out_specs=(P(None, "cells"), P(), P(), P(), P()),
        check_vma=False,
    )
```

```python
import functools
import math

import jax
import jax.numpy as jnp
from jax import lax
from jax.experimental import pallas as pl
from jax.experimental.pallas import tpu as pltpu
from jax.sharding import PartitionSpec as P

BF = jnp.bfloat16
F32 = jnp.float32
I16 = jnp.int16
I32 = jnp.int32
VARS = 8
GRID_ROWS = 8
TILE_ROWS = 16
TILE_WIDTH = 256

def onehot(h, n):
    it = lax.broadcasted_iota(I16, (n, h.shape[1]), 0)
    hh = jnp.broadcast_to(h.astype(I16), (n, h.shape[1]))
    return jnp.where(it == hh, jnp.ones((), BF), jnp.zeros((), BF))

def picktree(mm, lo, count):
    l8 = jnp.broadcast_to(lo, (8, lo.shape[1]))
    masks = {}
    c = count // 2
    while c:
        masks[c] = (l8 & c) != 0
        c //= 2
    def tree(base, n):
        if n == 1: return mm[8*base:8*base+8]
        h = n // 2
        a = tree(base, h); b = tree(base+h, h)
        return jnp.where(masks[h], b, a)
    return tree(0, count)

def k1c_body(ll_ref, rows_ref, out_ref, tab_ref):
    @pl.when(pl.program_id(0) == 0)
    def _():
        for k in range(16):
            a = ll_ref[:, 1024*k:1024*k+512]; b = ll_ref[:, 1024*k+512:1024*k+1024]
            tab_ref[16*k:16*k+16, :] = jnp.concatenate([a, b], axis=0)
    for j in range(4):
        outs = []
        for u in range(2):
            idx = rows_ref[2*j+u:2*j+u+1, :]
            mm = jnp.dot(tab_ref[...], onehot(idx & 511, 512), preferred_element_type=F32)
            outs.append(picktree(mm, idx >> 9, 32))
        out_ref[16*j:16*j+16, :] = jnp.concatenate(outs, 0).astype(BF)

def k1c(ll, rows):
    return pl.pallas_call(k1c_body, grid=(16,),
        in_specs=[pl.BlockSpec((8,16384), lambda i:(0,0)), pl.BlockSpec((8,512), lambda i:(i,0))],
        out_specs=pl.BlockSpec((64,512), lambda i:(i,0)),
        out_shape=jax.ShapeDtypeStruct((1024,512), BF),
        scratch_shapes=[pltpu.VMEM((256,512), BF)], name="k1")(ll, rows)

def gelu_both(x):
    c = math.sqrt(2 / math.pi)
    x2 = x * x
    th = jnp.tanh(c * (x + 0.044715 * x2 * x))
    act = x * (0.5 * (1.0 + th))
    der = 0.5 * (1.0 + th) + 0.5 * x * (1.0 - th * th) * (c * (1.0 + 3 * 0.044715 * x2))
    return act, der

def nt(a, b):
    return lax.dot_general(a, b, (((1,), (1,)), ((), ())), preferred_element_type=F32)

def kf_body(reg_ref, lc_ref, rc_ref, up_ref, lw_ref, n0_ref, n1_ref, n2_ref, n3_ref, cw_ref, uw_ref, dw_ref, hw_ref, rows_ref,
            out_ref, st_ref, tab_ref):
    @pl.when(pl.program_id(0) == 0)
    def _():
        w = 256
        reg = reg_ref[...].astype(F32)
        pick_col = (lax.broadcasted_iota(I32, (16, 4096), 1) == 256 * lax.broadcasted_iota(I32, (16, 4096), 0))
        spread = jnp.where(pick_col, 1.0, 0.0).astype(BF)
        lcol = jnp.dot(lc_ref[...], spread, preferred_element_type=F32)
        rcol = pltpu.roll(jnp.dot(rc_ref[...], spread, preferred_element_type=F32), 255, 1)
        col = lax.broadcasted_iota(I32, (8, 4096), 1) & 255
        left = jnp.where(col == 0, lcol, pltpu.roll(reg, 1, 1))
        right = jnp.where(col == 255, rcol, pltpu.roll(reg, 4095, 1))
        def line(ref, swap_l, swap_r):
            x = ref[...].astype(F32)
            a, b, c = x[:, 0:w], x[:, 1:w+1], x[:, 2:w+2]
            lane = lax.broadcasted_iota(I32, (8, w), 1)
            a = jnp.where((lane == 0) & swap_l, b, a)
            c = jnp.where((lane == w-1) & swap_r, b, c)
            return a, b, c
        ups = line(up_ref, n0_ref[0:1, 0:1] != 0, n1_ref[2:3, 127:128] != 257)
        lows = line(lw_ref, n2_ref[6:7, 0:1] != 17*258, n3_ref[8:9, 127:128] != 17*258+257)
        for dc, mid in enumerate((left, reg, right)):
            full = jnp.concatenate([ups[dc], mid, lows[dc]], axis=1).astype(BF)
            for dr in range(3):
                st_ref[(dr*3+dc)*8:(dr*3+dc)*8+8, :] = full[:, dr*w:dr*w+4096]
        def chunk(j, c):
            s = st_ref[:, pl.ds(pl.multiple_of(j*512, 512), 512)]
            conv = jnp.dot(cw_ref[...], s, preferred_element_type=F32)
            pre = jnp.dot(uw_ref[...], conv.astype(BF), preferred_element_type=F32)
            act = jax.nn.gelu(pre).astype(BF)
            mixed = (conv + jnp.dot(dw_ref[...], act, preferred_element_type=F32)).astype(BF)
            head = jnp.dot(hw_ref[...], mixed, preferred_element_type=F32).astype(BF)
            tab_ref[pl.ds(pl.multiple_of(16*j,16),16), :] = jnp.concatenate([head[:, :256], head[:, 256:]], axis=0)
            return c
        lax.fori_loop(0, 8, chunk, 0)
    def part(k, c):
        rows = rows_ref[pl.ds(pl.multiple_of(16*k, 16), 16), :]
        for j in range(8):
            outs = []
            for u in range(2):
                idx = rows[2*j+u:2*j+u+1]
                mm = jnp.dot(tab_ref[...], onehot(idx & 255, 256), preferred_element_type=F32)
                outs.append(picktree(mm, idx >> 8, 16))
            out_ref[pl.ds(pl.multiple_of(128*k + 16*j, 16), 16), :] = jnp.concatenate(outs, 0).astype(BF)
        return c
    lax.fori_loop(0, 2, part, 0)

def kf(reg, lc, rc, up, lw, neigh, cw, uw, dw, hw, rows):
    fix = lambda s: pl.BlockSpec(s, lambda i: (0, 0))
    nb = lambda b: pl.BlockSpec((9, 128), lambda i: (0, b))
    return pl.pallas_call(kf_body, grid=(4,),
        in_specs=[fix((8,4096)), fix((8,16)), fix((8,16)), fix((8,258)), fix((8,258)), nb(0), nb(1), nb(30), nb(31),
                  fix((64,72)), fix((256,64)), fix((64,256)), fix((8,64)), pl.BlockSpec((32,512), lambda i:(i,0))],
        out_specs=[pl.BlockSpec((256,512), lambda i:(i,0)), fix((72,4096))],
        out_shape=[jax.ShapeDtypeStruct((1024,512), BF), jax.ShapeDtypeStruct((72,4096), BF)],
        scratch_shapes=[pltpu.VMEM((128,256), BF)], name="kf",
    )(reg, lc, rc, up, lw, neigh, neigh, neigh, neigh, cw, uw, dw, hw, rows)

def kr_body(st_ref, cw_ref, uw_ref, dw_ref, cb_ref, act_ref, der_ref, mix_ref):
    conv = jnp.dot(cw_ref[...], st_ref[...], preferred_element_type=F32)
    cb = conv.astype(BF)
    cb_ref[...] = cb
    act, der = gelu_both(jnp.dot(uw_ref[...], cb, preferred_element_type=F32))
    act = act.astype(BF)
    act_ref[...] = act
    der_ref[...] = der
    mix_ref[...] = (conv + jnp.dot(dw_ref[...], act, preferred_element_type=F32)).astype(BF)

def kr(st, cw, uw, dw):
    fix = lambda s: pl.BlockSpec(s, lambda i: (0, 0))
    col = lambda r: pl.BlockSpec((r, 512), lambda i: (0, i))
    return pl.pallas_call(kr_body, grid=(8,),
        in_specs=[col(72), fix((64,72)), fix((256,64)), fix((64,256))],
        out_specs=[col(64), col(256), col(256), col(64)],
        out_shape=[jax.ShapeDtypeStruct((64,4096), BF), jax.ShapeDtypeStruct((256,4096), BF), jax.ShapeDtypeStruct((256,4096), F32), jax.ShapeDtypeStruct((64,4096), BF)],
        name="kr", cost_estimate=pl.CostEstimate(flops=10**10, bytes_accessed=8*10**6, transcendentals=10**6),
    )(st, cw, uw, dw)

def kb_body(sg_ref, rows_ref, st_ref, cb_ref, act_ref, der_ref, mix_ref, ut_ref, dt_ref, ht_ref,
            out_ref, acc_ref, gd_ref, gu_ref, ch_ref, go_ref):
    i = pl.program_id(0)
    @pl.when(i == 0)
    def _():
        for ref in (acc_ref, gd_ref, gu_ref, ch_ref): ref[...] = jnp.zeros_like(ref)
    @pl.when(i < 4)
    def _():
        half = lax.broadcasted_iota(I16, (16, 4096), 0) >> 3
        z = jnp.zeros((), BF)
        def part(j, c):
            sg = sg_ref[pl.ds(pl.multiple_of(64*j, 64), 64), :]
            rows = rows_ref[pl.ds(pl.multiple_of(8*j, 8), 8), :]
            val = jnp.concatenate([sg[8*k:8*k+8] for k in range(8)], axis=1)
            idx = jnp.concatenate([rows[k:k+1] for k in range(8)], axis=1)
            val2 = jnp.concatenate([val, val], axis=0)
            q = jnp.broadcast_to((idx >> 8).astype(I16), (16, 4096)) - half
            e = jnp.concatenate([jnp.where(q == jnp.int16(2*k), val2, z) for k in range(8)], axis=0)
            hot = onehot(idx & 255, 256)
            acc_ref[...] += sum(nt(hot[:, 1024*k:1024*k+1024], e[:, 1024*k:1024*k+1024]) for k in range(4))
            return c
        lax.fori_loop(0, 4, part, 0)
        @pl.when(i == 3)
        def _(): go_ref[...] = acc_ref[...].T
    @pl.when(i >= 4)
    def _():
        a2 = go_ref[pl.ds(pl.multiple_of(16*(i-4),16),16), :]
        go = jnp.concatenate([a2[:8], a2[8:]], axis=1).astype(BF)
        gm = jnp.dot(ht_ref[...], go, preferred_element_type=F32)
        gmb = gm.astype(BF)
        ch_ref[:, 72:80] += nt(mix_ref[...], go)
        gp = (jnp.dot(dt_ref[...], gmb, preferred_element_type=F32) * der_ref[...]).astype(BF)
        gd_ref[...] += nt(gmb, act_ref[...])
        gu_ref[...] += nt(cb_ref[...], gp)
        gco = (gm + jnp.dot(ut_ref[...], gp, preferred_element_type=F32)).astype(BF)
        ch_ref[:, :72] += nt(gco, st_ref[...])
    @pl.when(i == pl.num_programs(0)-1)
    def _():
        p = lax.broadcasted_iota(I32, (128, 128), 0)
        q = lax.broadcasted_iota(I32, (128, 128), 1)
        v = (q * 57) >> 9
        perm = jnp.where(p == jnp.where(q < 72, (q - 9 * v) * 8 + v, q), 1.0, 0.0)
        out_ref[0:64] = gd_ref[:, :128]
        out_ref[64:128] = gd_ref[:, 128:]
        out_ref[128:192] = gu_ref[:, :128]
        out_ref[192:256] = gu_ref[:, 128:]
        out_ref[256:320] = jnp.dot(ch_ref[...], perm, precision=lax.Precision.HIGHEST, preferred_element_type=F32)
        out_ref[320:384] = jnp.zeros((64, 128), F32)

def kb(sg, rows, st, saved, uw, dw, hw):
    fix = lambda s: pl.BlockSpec(s, lambda i: (0, 0))
    col = lambda r: pl.BlockSpec((r, 512), lambda i: (0, jnp.maximum(i - 4, 0)))
    blk = lambda s: pl.BlockSpec(s, lambda i: (jnp.minimum(i, 3), 0))
    return pl.pallas_call(kb_body, grid=(12,),
        in_specs=[blk((256,512)), blk((32,512)), col(72), col(64), col(256), col(256), col(64), fix((64,256)), fix((256,64)), fix((64,8))],
        out_specs=fix((384,128)), out_shape=jax.ShapeDtypeStruct((384,128), F32),
        scratch_shapes=[pltpu.VMEM((256,128), F32), pltpu.VMEM((64,256), F32), pltpu.VMEM((64,256), F32), pltpu.VMEM((64,128), F32), pltpu.VMEM((128,256), F32)], name="kb",
    )(sg, rows, st, *saved, uw.T, dw.T, hw.T)

def unpack(whole):
    down = jnp.concatenate([whole[0:64], whole[64:128]], axis=1)
    up = jnp.concatenate([whole[128:192], whole[192:256]], axis=1).T
    return whole[256:320, :72], up, down, whole[256:320, 72:80].T

def prep_body(slot_ref, pos_ref, code_ref, gid_ref, ohp_ref):
    idx = jnp.concatenate([slot_ref[t:t+1, :] for t in range(4)], axis=1)
    d = idx >> 9
    g = (d * 147) >> 11
    it = lax.broadcasted_iota(I32, (16, 256), 0)
    hot = [jnp.where(it == g[:, 256*b:256*b+256], 1.0, 0.0) for b in range(16)]
    a = jnp.concatenate(hot, axis=0).astype(BF)
    sq = lambda f, n: jnp.where(f(lax.broadcasted_iota(I32, (n, n), 0), lax.broadcasted_iota(I32, (n, n), 1)), 1.0, 0.0).astype(BF)
    excl = jnp.dot(a, sq(lambda r, c: r < c, 256), preferred_element_type=F32)
    tot = jnp.dot(a, jnp.ones((256, 256), BF), preferred_element_type=F32)
    prefix = jnp.dot(sq(lambda r, c: ((r & 15) == (c & 15)) & (c < (r & ~15)), 256), tot.astype(BF), preferred_element_type=F32)
    count = prefix[240:256] + tot[240:256]
    nblk = ((count.astype(I32) + 255) >> 8).astype(F32)
    base = jnp.dot(sq(lambda r, c: c < r, 16), nblk.astype(BF), preferred_element_type=F32)
    lane = lax.broadcasted_iota(I32, (16, 256), 1)
    gid = jnp.sum(jnp.where(lane.astype(F32) >= base + nblk, 1.0, 0.0), axis=0, keepdims=True).astype(I32)
    used = jnp.sum(nblk, axis=0, keepdims=True).astype(I32)
    gid_ref[0] = jnp.where(lane[:1] == 255, used, jnp.minimum(gid, GROUPS - 1))
    first = 256.0 * base
    pos = jnp.concatenate([
        jnp.sum(hot[b] * (excl[16*b:16*b+16] + prefix[16*b:16*b+16] + first), axis=0, keepdims=True) for b in range(16)
    ], axis=1).astype(I32)
    pos_ref[0] = pos
    ohp_ref[...] = onehot(pos & 255, 256)
    z = jnp.zeros((), BF)
    q = jnp.broadcast_to((pos >> 8).astype(I16), (16, 4096)) - lax.broadcasted_iota(I16, (16, 4096), 0)
    code = (idx & 511) + ((d - SPAN * g) << 9)
    low = jnp.broadcast_to((code & 255).astype(F32), (16, 4096)).astype(BF)
    high = jnp.broadcast_to((code >> 8).astype(F32), (16, 4096)).astype(BF)
    e = jnp.concatenate([jnp.where(q == jnp.int16(16*k), v, z) for v in (low, high) for k in range(2)], axis=0)
    r = nt(ohp_ref[...], e).T
    code_ref[...] = (r[:32] + 256.0 * r[32:]).astype(I32)

def prep(slot, start, n):
    return pl.pallas_call(prep_body, grid=(n,),
        in_specs=[pl.BlockSpec((4,1024), lambda i:(0,i+start))],
        out_specs=[pl.BlockSpec((1,1,4096), lambda i:(i,0,0)), pl.BlockSpec((32,256), lambda i:(i,0)), pl.BlockSpec((1,1,256), lambda i:(i,0,0))],
        out_shape=[jax.ShapeDtypeStruct((n,1,4096), I32), jax.ShapeDtypeStruct((32*n,256), I32), jax.ShapeDtypeStruct((n,1,256), I32)],
        scratch_shapes=[pltpu.VMEM((256,4096), BF)], name="prep",
        cost_estimate=pl.CostEstimate(flops=n*1600000000, bytes_accessed=n*60000, transcendentals=0),
    )(slot)

def tree_pick(mm, lo, count):
    l8 = jnp.broadcast_to(lo, (8, lo.shape[1]))
    top = 1
    while top < count: top *= 2
    m = {}
    h = top // 2
    while h:
        m[h] = (l8 & h) != 0
        h //= 2
    def tree(base, n):
        if n == 1: return mm[8*base:8*base+8]
        h = n // 2
        if base + h >= count: return tree(base, h)
        return jnp.where(m[h], tree(base+h, h), tree(base, h))
    return tree(0, top)

def load_table(tab_ref, nat_ref):
    nat_ref[:1024] = tab_ref[...]
    nat_ref[1024:] = jnp.zeros((8*SPAN*GROUPS-1024, 512), BF)

def look_up(i, nb, nat_ref, code_ref, gid_ref, res_ref, oh_ref):
    half = nb // 2
    def go(j, c):
        for h in range(0, half, 2):
            outs = []
            for u in range(2):
                b = j*half + h + u
                code = code_ref[pl.ds(b, 1), :]
                oh = onehot(code & 511, 512)
                if oh_ref is not None: oh_ref[b] = oh
                at = pl.ds(pl.multiple_of(gid_ref[i, b] * (8*SPAN), 16), 8*SPAN)
                outs.append(tree_pick(jnp.dot(nat_ref[at, :], oh, preferred_element_type=F32), code >> 9, SPAN))
            res_ref[pl.ds(pl.multiple_of(8*(j*half+h), 16), 16), :] = jnp.concatenate(outs, axis=0).astype(BF)
        return c
    lax.fori_loop(0, 2, go, 0)

def blend(nb, pos_ref, w_ref, res_ref, ohp_ref, n):
    p = jnp.zeros((8, n), F32)
    for t in range(4):
        pos = pos_ref[0, :, t*n:(t+1)*n]
        ohp = onehot(pos & 255, 256)
        if ohp_ref is not None:
            ohp_ref[:, t*n:(t+1)*n] = ohp
        mm = jnp.dot(res_ref[:8*nb, :], ohp, preferred_element_type=F32)
        p = p + w_ref[t:t+1, :] * tree_pick(mm, pos >> 8, nb)
    return p

def k4_body(gid_ref, tab_ref, tgt_ref, w_ref, pos_ref, code_ref, pred_ref, send_ref,
            res_ref, oh_ref, ohp_ref, sv_ref, nat_ref, acc0_ref, acc1_ref):
    i = pl.program_id(0)
    n = 1024
    scale = 1.0 / math.sqrt(2097152)
    @pl.when(i == 0)
    def _():
        load_table(tab_ref, nat_ref)
        acc0_ref[...] = jnp.zeros_like(acc0_ref)
        acc1_ref[...] = jnp.zeros_like(acc1_ref)
    def run(nb):
        look_up(i, nb, nat_ref, code_ref, gid_ref, res_ref, oh_ref)
        pb = blend(nb, pos_ref, w_ref, res_ref, ohp_ref, n).astype(BF)
        pred_ref[...] = pb
        g = (pb.astype(F32) - tgt_ref[...].astype(F32)) * scale
        z = jnp.zeros((), BF)
        val = jnp.concatenate([(w_ref[t:t+1, :] * g).astype(BF) for t in range(4)], axis=1)
        val2 = jnp.concatenate([val, val], axis=0)
        row = lax.broadcasted_iota(I16, (16, 4*n), 0) >> 3
        q = jnp.broadcast_to((pos_ref[0] >> 8).astype(I16), (16, 4*n)) - row
        e = jnp.concatenate([jnp.where(q == jnp.int16(2*k), val2, z) for k in range(nb//2)], axis=0)
        sv_ref[:8*nb, :] = nt(ohp_ref[...], e).T.astype(BF)
        row = lax.broadcasted_iota(I16, (16, 256), 0) >> 3
        half = nb // 2
        def back(j, c):
            for h in range(0, half, 2):
                pair = sv_ref[pl.ds(pl.multiple_of(8*(j*half+h), 16), 16), :]
                for u, acc_ref in enumerate((acc0_ref, acc1_ref)):
                    b = j*half + h + u
                    vb = pair[8*u:8*u+8]
                    v2 = jnp.concatenate([vb, vb], axis=0)
                    q = jnp.broadcast_to((code_ref[pl.ds(b, 1), :] >> 9).astype(I16), (16, 256)) - row
                    eb = jnp.concatenate([jnp.where(q == jnp.int16(2*k), v2, z) for k in range(8)], axis=0)
                    acc_ref[gid_ref[i, b]] += nt(oh_ref[b], eb)
            return c
        lax.fori_loop(0, 2, back, 0)
    used = gid_ref[i, 255]
    @pl.when(used <= FEW)
    def _(): run(FEW)
    @pl.when(used > FEW)
    def _(): run(MANY)
    @pl.when(i == pl.num_programs(0)-1)
    def _():
        for g in range(GROUPS):
            rows = min(8*SPAN, 1024 - 8*SPAN*g)
            send_ref[8*SPAN*g:8*SPAN*g+rows, :] = (acc0_ref[g] + acc1_ref[g]).T[:rows].astype(BF)

def k4(tab, target, w, pos, code, gid):
    points = target.shape[1]
    rows = 8*SPAN*GROUPS
    return pl.pallas_call(k4_body, grid=(points//1024,),
        in_specs=[pl.BlockSpec(memory_space=pltpu.SMEM), pl.BlockSpec((1024,512), lambda i:(0,0)), pl.BlockSpec((8,1024), lambda i:(0,i)),
                  pl.BlockSpec((4,1024), lambda i:(0,i)), pl.BlockSpec((1,1,4096), lambda i:(i,0,0)), pl.BlockSpec((32,256), lambda i:(i,0))],
        out_specs=[pl.BlockSpec((8,1024), lambda i:(0,i)), pl.BlockSpec((1024,512), lambda i:(0,0))],
        out_shape=[jax.ShapeDtypeStruct((8,points), BF), jax.ShapeDtypeStruct((1024,512), BF)],
        scratch_shapes=[pltpu.VMEM((8*MANY,256), BF), pltpu.VMEM((MANY,512,256), BF), pltpu.VMEM((256,4096), BF), pltpu.VMEM((8*MANY,256), BF),
                        pltpu.VMEM((rows,512), BF), pltpu.VMEM((GROUPS,512,128), F32), pltpu.VMEM((GROUPS,512,128), F32)],
        name="k4", compiler_params=pltpu.CompilerParams(vmem_limit_bytes=60*2**20),
    )(gid.reshape(-1, 256), tab, target, w, pos, code)

def k2_body(gid_ref, tab_ref, w_ref, pos_ref, code_ref, out_ref, res_ref, nat_ref):
    i = pl.program_id(0)
    @pl.when(i == 0)
    def _(): load_table(tab_ref, nat_ref)
    def run(nb):
        look_up(i, nb, nat_ref, code_ref, gid_ref, res_ref, None)
        out_ref[...] = blend(nb, pos_ref, w_ref, res_ref, None, 1024).astype(BF)
    used = gid_ref[i, 255]
    @pl.when(used <= FEW)
    def _(): run(FEW)
    @pl.when(used > FEW)
    def _(): run(MANY)

def k2(tab, w, pos, code, gid):
    return pl.pallas_call(k2_body, grid=(4,),
        in_specs=[pl.BlockSpec(memory_space=pltpu.SMEM), pl.BlockSpec((1024,512), lambda i:(0,0)), pl.BlockSpec((4,1024), lambda i:(0,i)),
                  pl.BlockSpec((1,1,4096), lambda i:(i,0,0)), pl.BlockSpec((32,256), lambda i:(i,0))],
        out_specs=pl.BlockSpec((8,1024), lambda i:(0,i)),
        out_shape=jax.ShapeDtypeStruct((8,4096), BF),
        scratch_shapes=[pltpu.VMEM((8*MANY,256), BF), pltpu.VMEM((8*SPAN*GROUPS,512), BF)], name="k2",
    )(gid.reshape(-1, 256), tab, w, pos, code)


SPAN = 14
GROUPS = 10
FEW, MANY = 20, 28


def from_behind(value, by):
    devices = lax.axis_size("cells")
    return lax.ppermute(value, "cells", [(i, (i + by) % devices) for i in range(devices)])


def body(
    ll_fields, target, in_rows, in_slot, in_weight, neighbours, conv_weight, up_weight, down_weight,
    head_weight, out_rows, out_slot, out_weight,
):
    devices = lax.axis_size("cells")
    tile_cols = devices // GRID_ROWS
    exchange = functools.partial(
        lax.all_to_all, axis_name="cells", split_axis=0, concat_axis=0, tiled=True
    )
    in_plan = prep(in_slot, 0, 4)
    head_plan = prep(out_slot, 0, 7)
    received = exchange(k1c(ll_fields, in_rows[0]))
    received, head_plan = lax.optimization_barrier((received, head_plan))
    flat_reg = k2(received, in_weight, *in_plan)
    regridded = flat_reg.reshape(VARS, TILE_ROWS, TILE_WIDTH)
    left_col = from_behind(regridded[:, :, TILE_WIDTH - 1], 1)
    right_col = from_behind(regridded[:, :, 0], -1)
    last, first = TILE_ROWS - 1, 0
    line = lambda r: jnp.concatenate(
        [left_col[:, r : r + 1], regridded[:, r, :], right_col[:, r : r + 1]], axis=1
    )
    upper_line = from_behind(line(last), tile_cols)
    lower_line = from_behind(line(first), -tile_cols)
    conv_w = conv_weight.reshape(64, VARS, 9).transpose(0, 2, 1).reshape(64, 72)
    sending, stacked = kf(
        flat_reg, left_col, right_col, upper_line, lower_line, neighbours, conv_w, up_weight,
        down_weight, head_weight, out_rows[0],
    )
    arrived = exchange(sending)
    tail_plan = prep(out_slot, 7, 9)
    out_plan = [jnp.concatenate(pair, axis=0) for pair in zip(head_plan, tail_plan)]
    predicted, slot_grad = k4(arrived, target, out_weight, *out_plan)
    slot_grad, stacked = lax.optimization_barrier((slot_grad, stacked))
    saved = kr(stacked, conv_w, up_weight, down_weight)
    returned = exchange(slot_grad)
    packed = kb(returned, out_rows[0], stacked, saved, up_weight, down_weight, head_weight)
    flat = packed.reshape(devices, -1, 128)
    part = jnp.sum(exchange(flat), axis=0, keepdims=True)
    whole = exchange(jnp.broadcast_to(part, flat.shape)).reshape(packed.shape)
    return (predicted, *unpack(whole))


def solution(mesh):
    placed = (
        P(None, "cells"),
        P(None, "cells"),
        P("cells", None, None),
        P(None, "cells"),
        P(None, "cells"),
        P(None, "cells"),
        P(),
        P(),
        P(),
        P(),
        P("cells", None, None),
        P(None, "cells"),
        P(None, "cells"),
    )
    return jax.shard_map(
        body,
        mesh=mesh,
        in_specs=placed,
        out_specs=(P(None, "cells"), P(), P(), P(), P()),
        check_vma=False,
    )
```
